128 devices in a mesh: seq: 32 (over x, y, core), mp: 4 (over z).
Axes of the slice: x: 4, y: 4, z: 4, core: 2. Of those that a mesh axis runs over, the one named last changes fastest.
Arguments:
- values: bfloat16 [8192, 8192], P('seq', 'mp'), may hold values from -6 to 6
- k_first: bfloat16 [8192, 8192], P('seq', 'mp'), may hold values from -6 to 6
- q_first: bfloat16 [8192, 8192], P('seq', 'mp'), may hold values from -6 to 6
- k_second: bfloat16 [8192, 8192], P('seq', 'mp'), may hold values from -6 to 6
- q_second: bfloat16 [8192, 8192], P('seq', 'mp'), may hold values from -210 to 210
- mr_taps: bfloat16 [128, 8192], P(None, 'mp'), may hold values from -0.5 to 0.5
- li_rate: float32 [16, 8192], P(None, 'mp'), may hold values from 0 to 1, as said below
- li_residue: float32 [16, 8192], P(None, 'mp'), may hold values from -4 to 4
- tile_docs: int32 [64], replicated, may hold values from 0 to 7, never falling along the last dimension, each value on 1 to 32 neighbouring positions
Outputs:
- mixed: bfloat16 [8192, 8192], P('seq', 'mp')
The draws below stay inside these ranges and needn't reach their ends.
Inputs may be any that keep to these rules, and one draw needn't show every extreme that they name: `tile_docs`: ids never fall along the sequence; a document spans at most 32 tiles. `li_rate`: positive decay rates.
All inputs are finite; a program needn't handle non-finite values.
Results may differ from the reference program's by a relative error of at most 0.012.
Values may be sent and summed in bfloat16 or wider, within the bound.
A program may use at most 320 MiB of HBM per device.

```python
import math
import jax
import jax.numpy as jnp
import numpy as np
from jax import lax

D = 8192
TILE = 128
MR_TAPS = 128
MODES = 16
SEQ = 8192
NTILES = 64


def draw_q_second(key, part):
    key_a, key_b = jax.random.split(jax.random.fold_in(key, 11), 2)
    columns = jnp.arange(D, dtype=jnp.float32)
    col_scale = jnp.exp(jax.random.uniform(key_b, (1, D), minval=0.0, maxval=math.log(10.0)))
    col_scale = col_scale * jnp.exp(math.log(3.0) * columns / D)[None, :]
    raw_draw = jnp.clip(jax.random.normal(key_a, (SEQ, D)), -6.0, 6.0)
    return (raw_draw * col_scale).astype(jnp.bfloat16)


def draw_li_rate(key, part):
    key_a, key_b, key_c, key_d = jax.random.split(jax.random.fold_in(key, 23), 4)
    slow_cut = 0.35
    middle_cut = 0.65
    picker = jax.random.uniform(key_a, (MODES, D))
    slow_rate = jnp.exp(jax.random.uniform(key_b, (MODES, D), minval=math.log(0.05 / SEQ), maxval=math.log(1.0 / SEQ)))
    middle_rate = jnp.exp(jax.random.uniform(key_c, (MODES, D), minval=math.log(1.0 / SEQ), maxval=math.log(0.01)))
    fast_rate = jnp.exp(jax.random.uniform(key_d, (MODES, D), minval=math.log(0.02), maxval=math.log(0.05)))
    chosen = jnp.where(picker < slow_cut, slow_rate, jnp.where(picker < middle_cut, middle_rate, fast_rate))
    return chosen.astype(jnp.float32)


def block_scale(key, extent, pieces, smallest, top_value):
    def one(axis_at, shards_of):
        draws = jax.random.uniform(jax.random.fold_in(jax.random.fold_in(key, 6), axis_at), (shards_of,), jnp.float32, smallest / len(pieces), top_value / len(pieces))
        return jnp.repeat(jnp.exp(draws), extent[axis_at] // shards_of).reshape((-1,) + (1,) * (len(extent) - axis_at - 1))

    factor_of = one(*pieces[0])
    for cut in pieces[1:]:
        factor_of = factor_of * one(*cut)
    return factor_of


def split_up(count, total, bound, slope):
    portions = [(1 << 20) // math.isqrt(standing ** slope) + 1 for standing in range(2, count + 1)]
    surplus, counts = total - bound - (count - 1), [1] * (count - 1)
    while surplus > 0:
        free = [i for i in range(count - 1) if counts[i] < bound]
        mass, left = sum([portions[i] for i in free]), surplus
        for i in free:
            addition = min(bound - counts[i], max(1, left * portions[i] // mass), surplus)
            counts[i] = counts[i] + addition
            surplus = surplus - addition
    return np.array([bound] + counts)


def ragged(rng, count, total, reach, lean):
    if count == 2:
        one = jax.random.randint(rng, (), max(1, total - reach), min(reach, total - 1) + 1)
        return jnp.stack([one, total - one])
    sizes = jnp.asarray(split_up(count, total, reach, lean), jnp.int32)
    couples = (count - 1) // 2
    donor, taker = sizes[1:1 + 2 * couples:2], sizes[2:2 + 2 * couples:2]
    room = jnp.minimum(donor - 1, reach - taker)
    moved = jax.random.randint(jax.random.fold_in(rng, 1), (couples,), 0, 1 << 20) % (room + 1)
    sizes = sizes.at[1:1 + 2 * couples:2].set(donor - moved).at[2:2 + 2 * couples:2].set(taker + moved)
    return sizes[jax.random.permutation(jax.random.fold_in(rng, 2), count)]


def noise(key, extent, scale, most, cuts=(), kind=jnp.bfloat16):
    values = jax.random.normal(key, extent, jnp.float32) * scale
    if len(cuts) > 0:
        values = block_scale(key, extent, cuts, -0.22, 0.18) * values
    return jnp.clip(values, min=-most, max=most).astype(kind)


def setup_inputs(seed: int = 0) -> dict:
    key_list = jax.random.split(jax.random.key(seed), 10)
    return {
        "values": noise(key_list[0], (SEQ, D), 1.0, 6.0, ((0, 32), (1, 4))),
        "k_first": noise(key_list[1], (SEQ, D), 1.0, 6.0, ((0, 32), (1, 4))),
        "q_first": noise(key_list[2], (SEQ, D), 1.0, 6.0, ((0, 32), (1, 4))),
        "k_second": noise(key_list[3], (SEQ, D), 1.0, 6.0, ((0, 32), (1, 4))),
        "q_second": draw_q_second(jax.random.fold_in(key_list[9], 71), 0),
        "mr_taps": noise(key_list[5], (MR_TAPS, D), MR_TAPS ** -0.5, 0.5, ((1, 4),)),
        "li_rate": draw_li_rate(jax.random.fold_in(key_list[9], 71), 0),
        "li_residue": noise(key_list[7], (MODES, D), 0.25, 4.0, ((1, 4),), jnp.float32),
        "tile_docs": jnp.searchsorted(jnp.cumsum(ragged(key_list[8], NTILES // 8, NTILES, NTILES // 2, 2)), jnp.arange(NTILES), side="right").astype(jnp.int32),
    }


norm_eps = 1e-06
top_precision = lax.Precision.HIGHEST

def lag_tables():
    later = np.arange(TILE)[:, None]
    earlier = np.arange(TILE)[None, :]
    same_lag = later - earlier
    back_lag = TILE + later - earlier
    same_ok = same_lag >= 0
    back_ok = back_lag < TILE
    return (np.where(same_ok, same_lag, 0), same_ok, np.where(back_ok, back_lag, 0), back_ok)

def banded(taps, index_table, valid):
    return jnp.where(valid[:, :, None], taps[index_table], jnp.zeros((), taps.dtype))

def rounded(array_in):
    return lax.optimization_barrier(array_in.astype(jnp.bfloat16)).astype(jnp.float32)

def mode_tables(li_rate, li_residue):
    lag_steps = jnp.arange(TILE, dtype=jnp.float32)
    amplitude = li_residue * jnp.sqrt(li_rate)
    end_weights = jnp.exp(-li_rate[:, None, :] * (TILE - 1 - lag_steps)[None, :, None])
    out_weights = amplitude[None] * jnp.exp(-li_rate[None] * (lag_steps + 1.0)[:, None, None])
    filter_taps = lax.optimization_barrier(jnp.sum(amplitude[None] * jnp.exp(-li_rate[None] * lag_steps[:, None, None]), axis=1))
    decay = jnp.exp(-li_rate * TILE)
    return (end_weights, out_weights, filter_taps, decay)

def run_tiles(start_state, tile_ends, kept, decay):

    def advance(carried, scan_item):
        tile_end, kept_flag = scan_item
        entered = carried * kept_flag
        return (decay * entered + tile_end, entered)
    return lax.scan(advance, start_state, (tile_ends, kept))

def channel_group(values, k_first, q_first, k_second, q_second, mr_taps, li_rate, li_residue, kept):
    tile_count = values.shape[0] // TILE
    group_size = values.shape[1]
    shape_tiles = (tile_count, TILE, group_size)
    same_idx, same_ok, back_idx, back_ok = lag_tables()
    gated_in = rounded(k_first.astype(jnp.float32) * values.astype(jnp.float32))
    current = gated_in.reshape(shape_tiles)
    previous = jnp.concatenate([jnp.zeros((1, TILE, group_size), jnp.float32), current[:-1]], axis=0)
    taps_wide = mr_taps.astype(jnp.float32)
    conv_out = jnp.einsum('jic,nic->njc', banded(taps_wide, same_idx, same_ok), current, precision=top_precision)
    conv_out = conv_out + kept[:, None, None] * jnp.einsum('jic,nic->njc', banded(taps_wide, back_idx, back_ok), previous, precision=top_precision)
    short_out = rounded(q_first.astype(jnp.float32).reshape(shape_tiles) * conv_out)
    long_in = rounded(k_second.astype(jnp.float32).reshape(shape_tiles) * short_out)
    end_weights, out_weights, filter_taps, decay = mode_tables(li_rate, li_residue)
    inside = jnp.einsum('jic,nic->njc', banded(filter_taps, same_idx, same_ok), long_in, precision=top_precision)
    tile_ends = jnp.einsum('mjc,njc->nmc', end_weights, long_in, precision=top_precision)
    final_state, entering = run_tiles(jnp.zeros_like(decay), tile_ends, kept, decay)
    state_part = jnp.einsum('jmc,nmc->njc', out_weights, entering, precision=top_precision)
    long_out = q_second.astype(jnp.float32).reshape(shape_tiles) * (state_part + inside)
    return long_out.reshape(-1, group_size)

def reference(values, k_first, q_first, k_second, q_second, mr_taps, li_rate, li_residue, tile_docs):
    group_size = min(256, D)
    group_count = D // group_size
    kept = jnp.concatenate([jnp.zeros((1,), jnp.float32), (tile_docs[1:] == tile_docs[:-1]).astype(jnp.float32)])

    def split_cols(array_in):
        return jnp.moveaxis(array_in.reshape(array_in.shape[0], group_count, group_size), 1, 0)
    stacked = tuple((split_cols(array_in) for array_in in (values, k_first, q_first, k_second, q_second, mr_taps, li_rate, li_residue)))
    long_out = lax.map(lambda group_args: channel_group(*group_args, kept), stacked)
    long_out = jnp.moveaxis(long_out, 0, 1).reshape(SEQ, D)
    power = lax.optimization_barrier(jnp.mean(long_out * long_out, axis=1, keepdims=True))
    return (long_out * lax.rsqrt(power + norm_eps)).astype(jnp.bfloat16)
```

```python
import functools
import jax
import jax.numpy as jnp
import numpy as np
from jax import lax
from jax.experimental import pallas as pl
from jax.experimental.pallas import tpu as pltpu
from jax.sharding import PartitionSpec as P

TILE = 128
MODES = 16
LANES = 128
WIDE = 256
norm_eps = 1e-06
MESH = pl.DeviceIdType.MESH


def split_bf16(table):
    high = table.astype(jnp.bfloat16)
    low = (table - high.astype(np.float64)).astype(jnp.bfloat16)
    return np.asarray(high), np.asarray(low)


def dft_tables():
    freq = 2.0 * np.pi * (4.0 * np.arange(TILE) + 1.0) / (4.0 * TILE)
    angle = freq[:, None] * np.arange(TILE)[None, :]
    forward = np.concatenate([np.cos(angle), -np.sin(angle)], axis=0)
    inverse = forward.T / TILE
    f_high, f_low = split_bf16(forward)
    g_high, g_low = split_bf16(inverse)
    ahead = np.concatenate([f_high, f_low, f_high], axis=1)
    back = np.concatenate([g_high, g_low, g_high], axis=1)
    return ahead, back


def wait_bytes(ref, sem):
    pltpu.make_async_copy(ref, ref, sem).wait()


def kernel(
    seq_count, mp_count,
    docs, values_h, k1_h, q1_h, k2_h, q2_h, taps_h, rate_h, resid_h, ahead_h, back_h,
    out_h,
    values, k1, q1, k2, q2, taps, rate, resid, ahead, back,
    gated, halo, longin, inside, longout, amp, z8, z128, zb,
    acc1, ends0, esend, erecv, ssend, srecv, power, psend, precv, outbuf,
    in_sem, par_sem, halo_send, halo_recv, e_send, e_recv, s_send, s_recv, p_send, p_recv, out_sem,
):
    me = lax.axis_index("seq")
    part = lax.axis_index("mp")
    chunks = values.shape[1] // WIDE
    channels = values.shape[1]

    def in_copy(source, target, row, ch):
        cols = pl.ds(ch * WIDE, WIDE)
        return pltpu.make_async_copy(source.at[:, cols], target.at[:, cols], in_sem.at[row, ch])

    for ch in range(chunks):
        in_copy(values_h, values, 0, ch).start()
        in_copy(k1_h, k1, 1, ch).start()
    whole = [(rate_h, rate), (resid_h, resid), (taps_h, taps), (ahead_h, ahead), (back_h, back),
             (q1_h, q1), (k2_h, k2), (q2_h, q2)]
    whole_copies = [pltpu.make_async_copy(a, b, par_sem.at[n]) for n, (a, b) in enumerate(whole)]
    for copy in whole_copies:
        copy.start()

    barrier = pltpu.get_barrier_semaphore()

    def greet(step, carry):
        pl.semaphore_signal(barrier, inc=1, device_id=(lax.rem(me + step, seq_count), part), device_id_type=MESH)
        return carry

    lax.fori_loop(1, seq_count, greet, 0)
    for step in range(1, mp_count):
        pl.semaphore_signal(barrier, inc=1, device_id=(me, lax.rem(part + step, mp_count)), device_id_type=MESH)

    for ch in range(chunks):
        in_copy(values_h, values, 0, ch).wait()
        in_copy(k1_h, k1, 1, ch).wait()
        cols = pl.ds(ch * WIDE, WIDE)
        for half in (1, 0):
            rows = pl.ds(half * TILE, TILE)
            product = k1[rows, cols].astype(jnp.float32) * values[rows, cols].astype(jnp.float32)
            gated[half, ch] = product.astype(jnp.bfloat16)

    for copy in whole_copies[:2]:
        copy.wait()
    r_all = rate[...]
    amp[...] = resid[...] * jnp.sqrt(r_all)
    z8[...] = jnp.exp(-8.0 * r_all)
    z128[...] = jnp.exp(-float(TILE) * r_all)
    sub = lax.broadcasted_iota(jnp.int32, (8, LANES), 0).astype(jnp.float32)

    def fill_zb(group, carry):
        cols = pl.ds(pl.multiple_of(group * LANES, LANES), LANES)
        for m in range(MODES):
            zb[m, :, cols] = jnp.exp(-rate[m : m + 1, cols] * sub)
        return carry

    lax.fori_loop(0, channels // LANES, fill_zb, 0)

    pl.semaphore_wait(barrier, seq_count - 1 + mp_count - 1)
    after = lax.rem(me + 1, seq_count)

    def halo_copy(ch):
        return pltpu.make_async_remote_copy(
            src_ref=gated.at[1, ch], dst_ref=halo.at[ch], send_sem=halo_send, recv_sem=halo_recv.at[ch],
            device_id=(after, part), device_id_type=MESH)

    for ch in range(chunks):
        halo_copy(ch).start()

    first = 2 * me
    doc_before = docs[jnp.maximum(first - 1, 0)]
    doc_a = docs[first]
    doc_b = docs[first + 1]
    kept0 = jnp.where(jnp.logical_and(me > 0, doc_before == doc_a), 1.0, 0.0).astype(jnp.float32)
    kept1 = jnp.where(doc_a == doc_b, 1.0, 0.0).astype(jnp.float32)

    for copy in whole_copies[2:]:
        copy.wait()

    def transform(tile):
        doubled = jnp.concatenate([tile, tile], axis=0)
        return jnp.dot(ahead[:, : 2 * TILE], doubled, preferred_element_type=jnp.float32)

    def untransform(real, imag):
        real_high = real.astype(jnp.bfloat16)
        imag_high = imag.astype(jnp.bfloat16)
        real_low = (real - real_high.astype(jnp.float32)).astype(jnp.bfloat16)
        imag_low = (imag - imag_high.astype(jnp.float32)).astype(jnp.bfloat16)
        stacked = jnp.concatenate([real_high, imag_high, real_high, imag_high, real_low, imag_low], axis=0)
        return jnp.dot(back[...], stacked, preferred_element_type=jnp.float32)

    def short_tile(current, previous, kept, spectrum, rows, cols):
        real = current[:TILE] - kept * previous[TILE:]
        imag = current[TILE:] + kept * previous[:TILE]
        s_real, s_imag = spectrum[:TILE], spectrum[TILE:]
        conv = untransform(real * s_real - imag * s_imag, real * s_imag + imag * s_real)
        short = (q1[rows, cols].astype(jnp.float32) * conv).astype(jnp.bfloat16)
        return (k2[rows, cols].astype(jnp.float32) * short.astype(jnp.float32)).astype(jnp.bfloat16)

    def horner(tile, base):
        steps = [z8[m : m + 1, pl.ds(base, LANES)] for m in range(MODES)]
        sums = [tile[0:8]] * MODES
        for block in range(1, TILE // 8):
            row = tile[8 * block : 8 * block + 8]
            sums = [s * z + row for s, z in zip(sums, steps)]
        return sums

    def forward_chunk(ch, carry):
        start = pl.multiple_of(ch * WIDE, WIDE)
        cols = pl.ds(start, WIDE)
        spec0 = transform(gated[0, ch])
        spec1 = transform(gated[1, ch])
        spectrum = transform(taps[:, cols])
        late = short_tile(spec1, spec0, kept1, spectrum, pl.ds(TILE, TILE), cols)
        longin[1, ch] = late
        for group in range(2):
            wide = longin[1, ch, :, group * LANES : (group + 1) * LANES].astype(jnp.float32)
            for m, s in enumerate(horner(wide, start + group * LANES)):
                acc1[group, m] = s
        wait_bytes(halo.at[ch], halo_recv.at[ch])
        spec_h = transform(halo[ch])
        early = short_tile(spec0, spec_h, kept0, spectrum, pl.ds(0, TILE), cols)
        longin[0, ch] = early
        for group in range(2):
            base = start + group * LANES
            wide = longin[0, ch, :, group * LANES : (group + 1) * LANES].astype(jnp.float32)
            for m, s in enumerate(horner(wide, base)):
                weight = jnp.exp(-rate[m : m + 1, pl.ds(base, LANES)] * (7.0 - sub))
                decay = kept1 * z128[m : m + 1, pl.ds(base, LANES)]
                ends0[m : m + 1, pl.ds(base, LANES)] = jnp.sum(s * weight, axis=0, keepdims=True)
                both = (acc1[group, m] + decay * s) * weight
                esend[4 * ch + 2 * group + m // 8, m % 8 : m % 8 + 1, :] = jnp.sum(both, axis=0, keepdims=True)
        for piece in range(4):
            owner = 4 * ch + piece

            @pl.when(owner != me)
            def _():
                pltpu.make_async_remote_copy(
                    src_ref=esend.at[owner], dst_ref=erecv.at[me], send_sem=e_send, recv_sem=e_recv,
                    device_id=(owner, part), device_id_type=MESH).start()

            @pl.when(owner == me)
            def _():
                pltpu.make_async_copy(esend.at[owner], erecv.at[me], e_recv).start()

        return carry

    lax.fori_loop(0, chunks, forward_chunk, 0)

    def inside_chunk(ch, carry):
        start = pl.multiple_of(ch * WIDE, WIDE)
        highs, lows = [], []
        for group in range(2):
            base = start + group * LANES
            lanes = pl.ds(base, LANES)
            power_of = [amp[m : m + 1, lanes] * zb[m, :, lanes] for m in range(MODES)]
            steps = [z8[m : m + 1, lanes] for m in range(MODES)]
            pieces = []
            for block in range(TILE // 8):
                total = power_of[0]
                for p in power_of[1:]:
                    total = total + p
                pieces.append(total)
                if block < TILE // 8 - 1:
                    power_of = [p * z for p, z in zip(power_of, steps)]
            lag_taps = jnp.concatenate(pieces, axis=0)
            high = lag_taps.astype(jnp.bfloat16)
            highs.append(high)
            lows.append((lag_taps - high.astype(jnp.float32)).astype(jnp.bfloat16))
        high = jnp.concatenate(highs, axis=1)
        low = jnp.concatenate(lows, axis=1)
        stacked = jnp.concatenate([high, high, low], axis=0)
        spectrum = jnp.dot(ahead[...], stacked, preferred_element_type=jnp.float32)
        s_real, s_imag = spectrum[:TILE], spectrum[TILE:]
        for half in range(2):
            spec = transform(longin[half, ch])
            real, imag = spec[:TILE], spec[TILE:]
            inside[half, ch] = untransform(real * s_real - imag * s_imag, real * s_imag + imag * s_real)
        return carry

    lax.fori_loop(0, chunks, inside_chunk, 0)

    wait_bytes(erecv, e_recv)
    my_chip = me // 2
    my_cols = pl.ds(pl.multiple_of(my_chip * LANES, LANES), LANES)
    my_rate = rate[pl.ds(pl.multiple_of(8 * lax.rem(me, 2), 8), 8), my_cols]
    block_decay = jnp.exp(-2.0 * TILE * my_rate)

    def scan_step(n, state):
        ssend[n] = state
        before = docs[jnp.maximum(2 * n - 1, 0)]
        through = jnp.where(jnp.logical_and(n > 0, before == docs[2 * n + 1]), 1.0, 0.0).astype(jnp.float32)
        return (block_decay * through) * state + erecv[n]

    lax.fori_loop(0, seq_count, scan_step, jnp.zeros((8, LANES), jnp.float32))

    slot = me // 4

    def hand_back(step, carry):
        target = lax.rem(me + step, seq_count)
        pltpu.make_async_remote_copy(
            src_ref=ssend.at[target], dst_ref=srecv.at[me], send_sem=s_send, recv_sem=s_recv.at[slot],
            device_id=(target, part), device_id_type=MESH).start()
        return carry

    lax.fori_loop(1, seq_count, hand_back, 0)
    pltpu.make_async_copy(ssend.at[me], srecv.at[me], s_recv.at[slot]).start()

    power[...] = jnp.zeros_like(power)

    def outward_chunk(ch, carry):
        start = pl.multiple_of(ch * WIDE, WIDE)
        tiles = pl.ds(pl.multiple_of(4 * ch, 4), 4)
        wait_bytes(srecv.at[tiles], s_recv.at[ch])
        for group in range(2):
            base = start + group * LANES
            lanes = pl.ds(base, LANES)
            steps = [z8[m : m + 1, lanes] for m in range(MODES)]
            states = [kept0 * srecv[4 * ch + 2 * group + m // 8, m % 8 : m % 8 + 1, :] for m in range(MODES)]
            for half in range(2):
                if half == 1:
                    states = [
                        kept1 * (z128[m : m + 1, lanes] * s + ends0[m : m + 1, lanes])
                        for m, s in enumerate(states)
                    ]
                waves = []
                for m, s in enumerate(states):
                    first_step = jnp.exp(-rate[m : m + 1, lanes])
                    waves.append((amp[m : m + 1, lanes] * first_step * s) * zb[m, :, lanes])
                for block in range(TILE // 8):
                    total = inside[half, ch, 8 * block : 8 * block + 8, group * LANES : (group + 1) * LANES]
                    for w in waves:
                        total = total + w
                    rows = pl.ds(half * TILE + 8 * block, 8)
                    total = total * q2[rows, lanes].astype(jnp.float32)
                    longout[rows, lanes] = total
                    power[rows, :] = power[rows, :] + total * total
                    if block < TILE // 8 - 1:
                        waves = [w * z for w, z in zip(waves, steps)]
        return carry

    lax.fori_loop(0, chunks, outward_chunk, 0)

    psend[...] = jnp.zeros_like(psend)
    for half in range(2):
        turned = power[half * TILE : (half + 1) * TILE, :].T
        psend[half : half + 1, :] = jnp.sum(turned, axis=0, keepdims=True)
    for step in range(1, mp_count):
        pltpu.make_async_remote_copy(
            src_ref=psend, dst_ref=precv.at[part], send_sem=p_send, recv_sem=p_recv,
            device_id=(me, lax.rem(part + step, mp_count)), device_id_type=MESH).start()
    precv[part] = psend[...]
    others = pl.ds(0, mp_count - 1)
    wait_bytes(precv.at[others], p_recv)
    total = precv[0]
    for n in range(1, mp_count):
        total = total + precv[n]
    scale = lax.rsqrt(total / (channels * mp_count) + norm_eps)
    for half in range(2):
        column = jnp.broadcast_to(scale[half : half + 1, :], (TILE, LANES)).T
        rows = pl.ds(half * TILE, TILE)
        for group in range(channels // LANES):
            lanes = slice(group * LANES, (group + 1) * LANES)
            outbuf[rows, lanes] = (longout[rows, lanes] * column).astype(jnp.bfloat16)
        pltpu.make_async_copy(outbuf.at[rows], out_h.at[rows], out_sem.at[half]).start()

    for half in range(2):
        rows = pl.ds(half * TILE, TILE)
        pltpu.make_async_copy(outbuf.at[rows], out_h.at[rows], out_sem.at[half]).wait()
    wait_bytes(gated.at[1], halo_send)
    wait_bytes(esend.at[pl.ds(0, seq_count - 1)], e_send)
    wait_bytes(ssend.at[pl.ds(0, seq_count - 1)], s_send)
    wait_bytes(precv.at[others], p_send)


def on_device(mesh_sizes, values, k_first, q_first, k_second, q_second, mr_taps, li_rate, li_residue, tile_docs):
    seq_count, mp_count = mesh_sizes
    rows, channels = values.shape
    chunks = channels // WIDE
    ahead, back = dft_tables()
    f32, bf16 = jnp.float32, jnp.bfloat16
    vmem = pltpu.VMEM
    any_spec = pl.BlockSpec(memory_space=pl.ANY)
    big = vmem((rows, channels), bf16)
    dma = pltpu.SemaphoreType.DMA
    return pl.pallas_call(
        functools.partial(kernel, seq_count, mp_count),
        out_shape=jax.ShapeDtypeStruct((rows, channels), bf16),
        in_specs=[pl.BlockSpec(memory_space=pltpu.SMEM)] + [any_spec] * 10,
        out_specs=any_spec,
        scratch_shapes=[
            big, big, big, big, big,
            vmem((TILE, channels), bf16),
            vmem((MODES, channels), f32),
            vmem((MODES, channels), f32),
            vmem(ahead.shape, bf16),
            vmem(back.shape, bf16),
            vmem((2, chunks, TILE, WIDE), bf16),
            vmem((chunks, TILE, WIDE), bf16),
            vmem((2, chunks, TILE, WIDE), bf16),
            vmem((2, chunks, TILE, WIDE), f32),
            vmem((rows, channels), f32),
            vmem((MODES, channels), f32),
            vmem((MODES, channels), f32),
            vmem((MODES, channels), f32),
            vmem((MODES, 8, channels), f32),
            vmem((2, MODES, 8, LANES), f32),
            vmem((MODES, channels), f32),
            vmem((seq_count, 8, LANES), f32),
            vmem((seq_count, 8, LANES), f32),
            vmem((seq_count, 8, LANES), f32),
            vmem((seq_count, 8, LANES), f32),
            vmem((rows, LANES), f32),
            vmem((8, LANES), f32),
            vmem((mp_count, 8, LANES), f32),
            big,
            dma((2, chunks)),
            dma((8,)),
            dma,
            dma((chunks,)),
            dma, dma, dma,
            dma((chunks,)),
            dma, dma,
            dma((2,)),
        ],
        compiler_params=pltpu.CompilerParams(
            collective_id=0, has_side_effects=True, vmem_limit_bytes=60 * 1024 * 1024),
    )(tile_docs, values, k_first, q_first, k_second, q_second, mr_taps, li_rate, li_residue,
      jnp.asarray(ahead), jnp.asarray(back))


def solution(mesh):
    sizes = (mesh.shape["seq"], mesh.shape["mp"])
    block = P("seq", "mp")
    param = P(None, "mp")
    return jax.shard_map(
        functools.partial(on_device, sizes),
        mesh=mesh,
        in_specs=(block, block, block, block, block, param, param, param, P()),
        out_specs=block,
        check_vma=False,
    )
```

```python
import functools
import jax
import jax.numpy as jnp
import numpy as np
from jax import lax
from jax.experimental import pallas as pl
from jax.experimental.pallas import tpu as pltpu
from jax.sharding import PartitionSpec as P

TILE = 128
MODES = 16
LANES = 128
WIDE = 256
norm_eps = 1e-06
MESH = pl.DeviceIdType.MESH


def split_bf16(table):
    high = table.astype(jnp.bfloat16)
    low = (table - high.astype(np.float64)).astype(jnp.bfloat16)
    return np.asarray(high), np.asarray(low)


def dft_tables():
    freq = 2.0 * np.pi * (4.0 * np.arange(TILE) + 1.0) / (4.0 * TILE)
    angle = freq[:, None] * np.arange(TILE)[None, :]
    real, imag = np.cos(angle), -np.sin(angle)

    def mixed(top, bottom):
        blocks = [part.reshape(TILE // 16, 1, 16, TILE) for part in (top, bottom)]
        return np.concatenate(blocks, axis=1).reshape(2 * TILE, TILE)

    current = mixed(real, imag)
    c_high, c_low = split_bf16(current)
    p_high, p_low = split_bf16(mixed(-imag, real))
    g_high, g_low = split_bf16(current.T / TILE)
    ahead = np.concatenate([c_high, c_low, c_high], axis=1)
    pair = np.concatenate([c_high, p_high, c_low, p_low], axis=1)
    back = np.concatenate([g_high, g_low, g_high], axis=1)
    return ahead, pair, back


def wait_bytes(ref, sem):
    pltpu.make_async_copy(ref, ref, sem).wait()


def parts_of(spectrum):
    blocks = spectrum.reshape(TILE // 16, 2, 16, WIDE)
    return blocks[:, 0], blocks[:, 1]


def woven(real, imag):
    return jnp.stack([real, imag], axis=1).reshape(2 * TILE, WIDE)


def kernel(
    seq_count, mp_count,
    docs, values_h, k1_h, q1_h, k2_h, q2_h, taps_h, rate_h, resid_h, ahead_h, pair_h, back_h,
    outbuf,
    values, k1, q1, k2, q2, taps, rate, resid, ahead, pair, back,
    gated, masked, halo, longin, inside, longout, amp, z1, z8, z128, zb, zr,
    spectra, ends0, ends1, esend, erecv, ssend, srecv, power, psend, precv,
    in_sem, par_sem, halo_send, halo_recv, e_send, e_recv, s_send, s_recv, p_send, p_recv,
):
    me = lax.axis_index("seq")
    part = lax.axis_index("mp")
    channels = values.shape[1]
    chunks = channels // WIDE

    def in_copy(source, target, row, ch):
        cols = pl.ds(ch * WIDE, WIDE)
        return pltpu.make_async_copy(source.at[:, cols], target.at[:, cols], in_sem.at[row, ch])

    for ch in range(chunks):
        in_copy(values_h, values, 0, ch).start()
        in_copy(k1_h, k1, 1, ch).start()

    barrier = pltpu.get_barrier_semaphore()

    def greet(step, carry):
        pl.semaphore_signal(barrier, inc=1, device_id=(lax.rem(me + step, seq_count), part), device_id_type=MESH)
        return carry

    lax.fori_loop(1, seq_count, greet, 0)
    for step in range(1, mp_count):
        pl.semaphore_signal(barrier, inc=1, device_id=(me, lax.rem(part + step, mp_count)), device_id_type=MESH)

    whole = [(rate_h, rate), (resid_h, resid), (taps_h, taps), (ahead_h, ahead), (pair_h, pair), (back_h, back),
             (q1_h, q1), (k2_h, k2), (q2_h, q2)]
    whole_copies = [pltpu.make_async_copy(a, b, par_sem.at[n]) for n, (a, b) in enumerate(whole)]
    for copy in whole_copies:
        copy.start()

    first = 2 * me
    doc_a = docs[first]
    doc_b = docs[first + 1]

    def flag(test):
        return jnp.where(test, 1.0, 0.0).astype(jnp.float32)

    kept0 = flag(jnp.logical_and(me > 0, docs[jnp.maximum(first - 1, 0)] == doc_a))
    kept1 = flag(doc_a == doc_b)
    doc_after = docs[jnp.minimum(first + 2, 2 * seq_count - 1)]
    kept2 = flag(jnp.logical_and(me < seq_count - 1, doc_after == doc_b))

    for ch in range(chunks):
        in_copy(values_h, values, 0, ch).wait()
        in_copy(k1_h, k1, 1, ch).wait()
        cols = pl.ds(ch * WIDE, WIDE)
        rows = pl.ds(TILE, TILE)
        product = k1[rows, cols].astype(jnp.float32) * values[rows, cols].astype(jnp.float32)
        masked[1, ch] = (kept2 * product).astype(jnp.bfloat16)

    pl.semaphore_wait(barrier, seq_count - 1 + mp_count - 1)
    after = lax.rem(me + 1, seq_count)

    for ch in range(chunks):
        pltpu.make_async_remote_copy(
            src_ref=masked.at[1, ch], dst_ref=halo.at[ch], send_sem=halo_send, recv_sem=halo_recv.at[ch],
            device_id=(after, part), device_id_type=MESH).start()

    for ch in range(chunks):
        cols = pl.ds(ch * WIDE, WIDE)
        for half in (0, 1):
            rows = pl.ds(half * TILE, TILE)
            product = k1[rows, cols].astype(jnp.float32) * values[rows, cols].astype(jnp.float32)
            gated[half, ch] = product.astype(jnp.bfloat16)
            if half == 0:
                masked[0, ch] = (kept1 * product).astype(jnp.bfloat16)

    for copy in whole_copies[:2]:
        copy.wait()
    r_all = rate[...]
    amp[...] = resid[...] * jnp.sqrt(r_all)
    z1[...] = jnp.exp(-r_all)
    z8[...] = jnp.exp(-8.0 * r_all)
    z128[...] = jnp.exp(-float(TILE) * r_all)
    sub = lax.broadcasted_iota(jnp.int32, (8, LANES), 0).astype(jnp.float32)

    def fill_zb(group, carry):
        cols = pl.ds(pl.multiple_of(group * LANES, LANES), LANES)
        for m in range(MODES):
            zb[m, :, cols] = jnp.exp(-rate[m : m + 1, cols] * sub)
            zr[m, :, cols] = jnp.exp(-rate[m : m + 1, cols] * (7.0 - sub))
        return carry

    lax.fori_loop(0, channels // LANES, fill_zb, 0)

    for copy in whole_copies[2:]:
        copy.wait()

    def transform(tile):
        doubled = jnp.concatenate([tile, tile], axis=0)
        return jnp.dot(ahead[:, : 2 * TILE], doubled, preferred_element_type=jnp.float32)

    def convolve(spectrum, filter_spectrum):
        real, imag = parts_of(spectrum)
        s_real, s_imag = parts_of(filter_spectrum)
        product = woven(real * s_real - imag * s_imag, real * s_imag + imag * s_real)
        high = product.astype(jnp.bfloat16)
        low = (product - high.astype(jnp.float32)).astype(jnp.bfloat16)
        return jnp.dot(back[...], jnp.concatenate([high, high, low], axis=0), preferred_element_type=jnp.float32)

    def short_tile(half, ch, current, previous):
        cols = pl.ds(pl.multiple_of(ch * WIDE, WIDE), WIDE)
        rows = pl.ds(half * TILE, TILE)
        stacked = jnp.concatenate([current, previous, current, previous], axis=0)
        spectrum = jnp.dot(pair[...], stacked, preferred_element_type=jnp.float32)
        conv = convolve(spectrum, spectra[ch])
        short = (q1[rows, cols].astype(jnp.float32) * conv).astype(jnp.bfloat16)
        longin[half, ch] = (k2[rows, cols].astype(jnp.float32) * short.astype(jnp.float32)).astype(jnp.bfloat16)

    def tile_ends(half, ch, ends):
        for group in range(WIDE // LANES):
            lanes = pl.ds(pl.multiple_of(ch * WIDE, WIDE) + group * LANES, LANES)
            tile = longin[half, ch, :, group * LANES : (group + 1) * LANES].astype(jnp.float32)
            steps = [z8[m : m + 1, lanes] for m in range(MODES)]
            sums = [tile[0:8]] * MODES
            for block in range(1, TILE // 8):
                row = tile[8 * block : 8 * block + 8]
                sums = [s * z + row for s, z in zip(sums, steps)]
            for m, s in enumerate(sums):
                ends[m : m + 1, lanes] = jnp.sum(s * zr[m, :, lanes], axis=0, keepdims=True)

    def late_conv(ch):
        spectra[ch] = transform(taps[:, pl.ds(pl.multiple_of(ch * WIDE, WIDE), WIDE)])
        short_tile(1, ch, gated[1, ch], masked[0, ch])

    def late_chunk(ch, carry):
        tile_ends(1, ch - 1, ends1)
        late_conv(ch)
        return carry

    late_conv(0)
    lax.fori_loop(1, chunks, late_chunk, 0)
    tile_ends(1, chunks - 1, ends1)

    def early_conv(ch):
        short_tile(0, ch, gated[0, ch], halo[ch])

    def send_ends(ch):
        for piece in range(4):
            owner = 4 * ch + piece
            lanes = pl.ds(pl.multiple_of(ch * WIDE, WIDE) + (piece // 2) * LANES, LANES)
            modes = pl.ds(8 * (piece % 2), 8)
            esend[owner] = ends1[modes, lanes] + kept1 * z128[modes, lanes] * ends0[modes, lanes]
        for piece in range(4):
            owner = 4 * ch + piece

            @pl.when(owner != me)
            def _():
                pltpu.make_async_remote_copy(
                    src_ref=esend.at[owner], dst_ref=erecv.at[me], send_sem=e_send, recv_sem=e_recv,
                    device_id=(owner, part), device_id_type=MESH).start()

    def early_chunk(ch, carry):
        wait_bytes(halo.at[ch], halo_recv.at[ch])
        tile_ends(0, ch - 1, ends0)
        early_conv(ch)
        send_ends(ch - 1)
        return carry

    wait_bytes(halo.at[0], halo_recv.at[0])
    early_conv(0)
    lax.fori_loop(1, chunks, early_chunk, 0)
    tile_ends(0, chunks - 1, ends0)
    send_ends(chunks - 1)
    pltpu.make_async_copy(esend.at[me], erecv.at[me], e_recv).start()

    def inside_chunk(ch, carry):
        start = pl.multiple_of(ch * WIDE, WIDE)
        highs, lows = [], []
        for group in range(2):
            lanes = pl.ds(start + group * LANES, LANES)
            power_of = [amp[m : m + 1, lanes] * zb[m, :, lanes] for m in range(MODES)]
            steps = [z8[m : m + 1, lanes] for m in range(MODES)]
            pieces = []
            for block in range(TILE // 8):
                total = power_of[0]
                for p in power_of[1:]:
                    total = total + p
                pieces.append(total)
                if block < TILE // 8 - 1:
                    power_of = [p * z for p, z in zip(power_of, steps)]
            lag_taps = jnp.concatenate(pieces, axis=0)
            high = lag_taps.astype(jnp.bfloat16)
            highs.append(high)
            lows.append((lag_taps - high.astype(jnp.float32)).astype(jnp.bfloat16))
        high = jnp.concatenate(highs, axis=1)
        low = jnp.concatenate(lows, axis=1)
        stacked = jnp.concatenate([high, high, low], axis=0)
        spectrum = jnp.dot(ahead[...], stacked, preferred_element_type=jnp.float32)
        for half in range(2):
            inside[half, ch] = convolve(transform(longin[half, ch]), spectrum)
        return carry

    lax.fori_loop(0, chunks // 2, inside_chunk, 0)

    wait_bytes(erecv, e_recv)
    my_cols = pl.ds(pl.multiple_of((me // 2) * LANES, LANES), LANES)
    my_rate = rate[pl.ds(pl.multiple_of(8 * lax.rem(me, 2), 8), 8), my_cols]
    block_decay = jnp.exp(-2.0 * TILE * my_rate)

    def scan_step(n, state):
        ssend[n] = state
        through = flag(jnp.logical_and(n > 0, docs[jnp.maximum(2 * n - 1, 0)] == docs[2 * n + 1]))
        return (block_decay * through) * state + erecv[n]

    lax.fori_loop(0, seq_count, scan_step, jnp.zeros((8, LANES), jnp.float32))

    slot = me // 4

    def hand_back(step, carry):
        target = lax.rem(me + step, seq_count)
        pltpu.make_async_remote_copy(
            src_ref=ssend.at[target], dst_ref=srecv.at[me], send_sem=s_send, recv_sem=s_recv.at[slot],
            device_id=(target, part), device_id_type=MESH).start()
        return carry

    lax.fori_loop(1, seq_count, hand_back, 0)
    pltpu.make_async_copy(ssend.at[me], srecv.at[me], s_recv.at[slot]).start()

    lax.fori_loop(chunks // 2, chunks, inside_chunk, 0)

    power[...] = jnp.zeros_like(power)

    def outward_chunk(ch, carry):
        start = pl.multiple_of(ch * WIDE, WIDE)
        tiles = pl.ds(pl.multiple_of(4 * ch, 4), 4)
        wait_bytes(srecv.at[tiles], s_recv.at[ch])
        for group in range(2):
            lanes = pl.ds(start + group * LANES, LANES)
            steps = [z8[m : m + 1, lanes] for m in range(MODES)]
            states = [kept0 * srecv[4 * ch + 2 * group + n] for n in range(2)]
            for half in range(2):
                if half == 1:
                    states = [
                        kept1 * (z128[8 * n : 8 * n + 8, lanes] * s + ends0[8 * n : 8 * n + 8, lanes])
                        for n, s in enumerate(states)
                    ]
                begun = [amp[8 * n : 8 * n + 8, lanes] * z1[8 * n : 8 * n + 8, lanes] * s for n, s in enumerate(states)]
                waves = [begun[m // 8][m % 8 : m % 8 + 1] * zb[m, :, lanes] for m in range(MODES)]
                for block in range(TILE // 8):
                    total = inside[half, ch, 8 * block : 8 * block + 8, group * LANES : (group + 1) * LANES]
                    for w in waves:
                        total = total + w
                    rows = pl.ds(half * TILE + 8 * block, 8)
                    total = total * q2[rows, lanes].astype(jnp.float32)
                    longout[rows, lanes] = total
                    power[rows, :] = power[rows, :] + total * total
                    if block < TILE // 8 - 1:
                        waves = [w * z for w, z in zip(waves, steps)]
        return carry

    lax.fori_loop(0, chunks, outward_chunk, 0)

    psend[...] = jnp.zeros_like(psend)
    for half in range(2):
        turned = power[half * TILE : (half + 1) * TILE, :].T
        psend[half : half + 1, :] = jnp.sum(turned, axis=0, keepdims=True)
    for step in range(1, mp_count):
        pltpu.make_async_remote_copy(
            src_ref=psend, dst_ref=precv.at[part], send_sem=p_send, recv_sem=p_recv,
            device_id=(me, lax.rem(part + step, mp_count)), device_id_type=MESH).start()
    precv[part] = psend[...]
    others = pl.ds(0, mp_count - 1)
    wait_bytes(precv.at[others], p_recv)
    total = precv[0]
    for n in range(1, mp_count):
        total = total + precv[n]
    scale = lax.rsqrt(total / (channels * mp_count) + norm_eps)
    for half in range(2):
        column = jnp.broadcast_to(scale[half : half + 1, :], (TILE, LANES)).T
        rows = pl.ds(half * TILE, TILE)
        for group in range(channels // LANES):
            lanes = slice(group * LANES, (group + 1) * LANES)
            outbuf[rows, lanes] = (longout[rows, lanes] * column).astype(jnp.bfloat16)

    wait_bytes(masked.at[1], halo_send)
    wait_bytes(esend.at[pl.ds(0, seq_count - 1)], e_send)
    wait_bytes(ssend.at[pl.ds(0, seq_count - 1)], s_send)
    wait_bytes(precv.at[others], p_send)


def on_device(mesh_sizes, values, k_first, q_first, k_second, q_second, mr_taps, li_rate, li_residue, tile_docs):
    seq_count, mp_count = mesh_sizes
    rows, channels = values.shape
    chunks = channels // WIDE
    ahead, pair, back = dft_tables()
    f32, bf16 = jnp.float32, jnp.bfloat16
    vmem = pltpu.VMEM
    hbm_spec = pl.BlockSpec(memory_space=pltpu.MemorySpace.HBM)
    big = vmem((rows, channels), bf16)
    modal = vmem((MODES, channels), f32)
    tiles = vmem((seq_count, 8, LANES), f32)
    dma = pltpu.SemaphoreType.DMA
    return pl.pallas_call(
        functools.partial(kernel, seq_count, mp_count),
        out_shape=vmem((rows, channels), bf16),
        in_specs=[pl.BlockSpec(memory_space=pltpu.SMEM)] + [hbm_spec] * 11,
        out_specs=pl.BlockSpec(memory_space=pltpu.VMEM),
        scratch_shapes=[
            big, big, big, big, big,
            vmem((TILE, channels), bf16),
            modal, modal,
            vmem(ahead.shape, bf16),
            vmem(pair.shape, bf16),
            vmem(back.shape, bf16),
            vmem((2, chunks, TILE, WIDE), bf16),
            vmem((2, chunks, TILE, WIDE), bf16),
            vmem((chunks, TILE, WIDE), bf16),
            vmem((2, chunks, TILE, WIDE), bf16),
            vmem((2, chunks, TILE, WIDE), f32),
            vmem((rows, channels), f32),
            modal, modal, modal, modal,
            vmem((MODES, 8, channels), f32),
            vmem((MODES, 8, channels), f32),
            vmem((chunks, 2 * TILE, WIDE), f32),
            modal, modal,
            tiles, tiles, tiles, tiles,
            vmem((rows, LANES), f32),
            vmem((8, LANES), f32),
            vmem((mp_count, 8, LANES), f32),
            dma((2, chunks)),
            dma((9,)),
            dma,
            dma((chunks,)),
            dma, dma, dma,
            dma((chunks,)),
            dma, dma,
        ],
        compiler_params=pltpu.CompilerParams(
            collective_id=0, has_side_effects=True, vmem_limit_bytes=56 * 1024 * 1024),
    )(tile_docs, values, k_first, q_first, k_second, q_second, mr_taps, li_rate, li_residue,
      jnp.asarray(ahead), jnp.asarray(pair), jnp.asarray(back))


def solution(mesh):
    sizes = (mesh.shape["seq"], mesh.shape["mp"])
    block = P("seq", "mp")
    param = P(None, "mp")
    return jax.shard_map(
        functools.partial(on_device, sizes),
        mesh=mesh,
        in_specs=(block, block, block, block, block, param, param, param, P()),
        out_specs=block,
        check_vma=False,
    )
```

```python
import functools
import jax
import jax.numpy as jnp
import numpy as np
from jax import lax
from jax.experimental import pallas as pl
from jax.experimental.pallas import tpu as pltpu
from jax.sharding import PartitionSpec as P

TILE = 128
MODES = 16
LANES = 128
WIDE = 256
norm_eps = 1e-06
MESH = pl.DeviceIdType.MESH


def split_bf16(table):
    high = table.astype(jnp.bfloat16)
    low = (table - high.astype(np.float64)).astype(jnp.bfloat16)
    return np.asarray(high), np.asarray(low)


def dft_tables():
    freq = 2.0 * np.pi * (4.0 * np.arange(TILE) + 1.0) / (4.0 * TILE)
    angle = freq[:, None] * np.arange(TILE)[None, :]
    real, imag = np.cos(angle), -np.sin(angle)

    def mixed(top, bottom):
        blocks = [part.reshape(TILE // 16, 1, 16, TILE) for part in (top, bottom)]
        return np.concatenate(blocks, axis=1).reshape(2 * TILE, TILE)

    current = mixed(real, imag)
    c_high, c_low = split_bf16(current)
    p_high, p_low = split_bf16(mixed(-imag, real))
    g_high, g_low = split_bf16(current.T / TILE)
    ahead = np.concatenate([c_high, c_low, c_high], axis=1)
    pair = np.concatenate([c_high, p_high, c_low, p_low], axis=1)
    back = np.concatenate([g_high, g_low], axis=0)
    return ahead, pair, back


def wait_bytes(ref, sem):
    pltpu.make_async_copy(ref, ref, sem).wait()


def parts_of(spectrum):
    blocks = spectrum.reshape(TILE // 16, 2, 16, WIDE)
    return blocks[:, 0], blocks[:, 1]


def woven(real, imag):
    return jnp.stack([real, imag], axis=1).reshape(2 * TILE, WIDE)


def kernel(
    seq_count, mp_count,
    docs, values_h, k1_h, q1_h, k2_h, q2_h, taps_h, rate_h, resid_h, ahead_h, pair_h, back_h,
    outbuf,
    values, k1, q1, k2, q2, taps, rate, resid, ahead, pair, back,
    gated, behind, outgoing, longin, inside, longout, amp, z1, z8, z128, zb, zr,
    spectra, parts, ends, esend, erecv, ssend, srecv, power, psend, precv,
    in_sem, par_sem, halo_send, halo_recv, e_send, e_recv, s_send, s_recv, p_send, p_recv,
):
    me = lax.axis_index("seq")
    part = lax.axis_index("mp")
    channels = values.shape[1]
    chunks = channels // WIDE

    def in_copy(source, target, row, ch):
        cols = pl.ds(ch * WIDE, WIDE)
        return pltpu.make_async_copy(source.at[:, cols], target.at[:, cols], in_sem.at[row, ch])

    for ch in range(chunks):
        in_copy(values_h, values, 0, ch).start()
        in_copy(k1_h, k1, 1, ch).start()

    barrier = pltpu.get_barrier_semaphore()

    def greet(step, carry):
        pl.semaphore_signal(barrier, inc=1, device_id=(lax.rem(me + step, seq_count), part), device_id_type=MESH)
        return carry

    lax.fori_loop(1, seq_count, greet, 0)
    for step in range(1, mp_count):
        pl.semaphore_signal(barrier, inc=1, device_id=(me, lax.rem(part + step, mp_count)), device_id_type=MESH)

    whole = [(rate_h, rate), (resid_h, resid), (taps_h, taps), (ahead_h, ahead), (pair_h, pair), (back_h, back),
             (q1_h, q1), (k2_h, k2), (q2_h, q2)]
    whole_copies = [pltpu.make_async_copy(a, b, par_sem.at[n]) for n, (a, b) in enumerate(whole)]
    for copy in whole_copies:
        copy.start()

    first = 2 * me
    doc_a = docs[first]
    doc_b = docs[first + 1]

    def flag(test):
        return jnp.where(test, 1.0, 0.0).astype(jnp.float32)

    kept0 = flag(jnp.logical_and(me > 0, docs[jnp.maximum(first - 1, 0)] == doc_a))
    kept1 = flag(doc_a == doc_b)
    doc_after = docs[jnp.minimum(first + 2, 2 * seq_count - 1)]
    kept2 = flag(jnp.logical_and(me < seq_count - 1, doc_after == doc_b))

    for ch in range(chunks):
        in_copy(values_h, values, 0, ch).wait()
        in_copy(k1_h, k1, 1, ch).wait()
        cols = pl.ds(ch * WIDE, WIDE)
        rows = pl.ds(TILE, TILE)
        product = k1[rows, cols].astype(jnp.float32) * values[rows, cols].astype(jnp.float32)
        gated[1, ch] = product.astype(jnp.bfloat16)
        outgoing[ch] = (kept2 * product).astype(jnp.bfloat16)

    pl.semaphore_wait(barrier, seq_count - 1 + mp_count - 1)
    after = lax.rem(me + 1, seq_count)

    for ch in range(chunks):
        pltpu.make_async_remote_copy(
            src_ref=outgoing.at[ch], dst_ref=behind.at[0, ch], send_sem=halo_send, recv_sem=halo_recv.at[ch],
            device_id=(after, part), device_id_type=MESH).start()

    for ch in range(chunks):
        cols = pl.ds(ch * WIDE, WIDE)
        rows = pl.ds(0, TILE)
        product = k1[rows, cols].astype(jnp.float32) * values[rows, cols].astype(jnp.float32)
        gated[0, ch] = product.astype(jnp.bfloat16)
        behind[1, ch] = (kept1 * product).astype(jnp.bfloat16)

    for copy in whole_copies[:2]:
        copy.wait()
    r_all = rate[...]
    amp[...] = resid[...] * jnp.sqrt(r_all)
    z1[...] = jnp.exp(-r_all)
    z8[...] = jnp.exp(-8.0 * r_all)
    z128[...] = jnp.exp(-float(TILE) * r_all)
    sub = lax.broadcasted_iota(jnp.int32, (8, WIDE), 0).astype(jnp.float32)

    def fill_zb(ch, carry):
        cols = pl.ds(pl.multiple_of(ch * WIDE, WIDE), WIDE)
        for m in range(MODES):
            zb[m, :, cols] = jnp.exp(-rate[m : m + 1, cols] * sub)
            zr[m, :, cols] = jnp.exp(-rate[m : m + 1, cols] * (7.0 - sub))
        return carry

    lax.fori_loop(0, chunks, fill_zb, 0)

    for copy in whole_copies[2:]:
        copy.wait()

    def transform(tile):
        doubled = jnp.concatenate([tile, tile], axis=0)
        return jnp.dot(ahead[:, : 2 * TILE], doubled, preferred_element_type=jnp.float32)

    def product_of(spectrum, filter_spectrum):
        real, imag = parts_of(spectrum)
        s_real, s_imag = parts_of(filter_spectrum)
        product = woven(real * s_real - imag * s_imag, real * s_imag + imag * s_real)
        high = product.astype(jnp.bfloat16)
        low = (product - high.astype(jnp.float32)).astype(jnp.bfloat16)
        return high, low

    def invert(high, low):
        both = jnp.dot(back[...], high, preferred_element_type=jnp.float32)
        fine = jnp.dot(back[:TILE], low, preferred_element_type=jnp.float32)
        return both[:TILE] + (both[TILE:] + fine)

    def convolve(spectrum, filter_spectrum):
        return invert(*product_of(spectrum, filter_spectrum))

    def place_of(step):
        half = 1 - step // chunks
        ch = lax.rem(step, chunks)
        return half, ch, pl.multiple_of(ch * WIDE, WIDE)

    def begin_tile(step):
        half, ch, start = place_of(step)
        current, previous = gated[half, ch], behind[half, ch]
        stacked = jnp.concatenate([current, previous, current, previous], axis=0)
        spectrum = jnp.dot(pair[...], stacked, preferred_element_type=jnp.float32)
        return spectrum, spectra[ch]

    def keep_parts(begun):
        parts[0], parts[1] = product_of(*begun)

    def finish_tile(step, conv):
        half, ch, start = place_of(step)
        cols = pl.ds(start, WIDE)
        rows = pl.ds(pl.multiple_of(half * TILE, TILE), TILE)
        short = (q1[rows, cols].astype(jnp.float32) * conv).astype(jnp.bfloat16)
        longin[half, ch] = (k2[rows, cols].astype(jnp.float32) * short.astype(jnp.float32)).astype(jnp.bfloat16)

    def tile_ends(step, groups):
        half, ch, start = place_of(step)
        for group in groups:
            lanes = pl.ds(start + group * LANES, LANES)
            tile = longin[half, ch, :, group * LANES : (group + 1) * LANES].astype(jnp.float32)
            steps = [z8[m : m + 1, lanes] for m in range(MODES)]
            sums = [tile[0:8]] * MODES
            for block in range(1, TILE // 8):
                row = tile[8 * block : 8 * block + 8]
                sums = [s * z + row for s, z in zip(sums, steps)]
            for m, s in enumerate(sums):
                ends[half, m : m + 1, lanes] = jnp.sum(s * zr[m, :, lanes], axis=0, keepdims=True)

    def tap_chunk(ch, carry):
        spectra[ch] = transform(taps[:, pl.ds(pl.multiple_of(ch * WIDE, WIDE), WIDE)])
        return carry

    def send_ends(ch):
        for piece in range(4):
            owner = 4 * ch + piece
            lanes = pl.ds(pl.multiple_of(ch * WIDE, WIDE) + (piece // 2) * LANES, LANES)
            modes = pl.ds(8 * (piece % 2), 8)
            esend[owner] = ends[1, modes, lanes] + kept1 * z128[modes, lanes] * ends[0, modes, lanes]
        for piece in range(4):
            owner = 4 * ch + piece

            @pl.when(owner != me)
            def _():
                pltpu.make_async_remote_copy(
                    src_ref=esend.at[owner], dst_ref=erecv.at[me], send_sem=e_send, recv_sem=e_recv,
                    device_id=(owner, part), device_id_type=MESH).start()

    def forward_step(step, carry):
        @pl.when(step + 1 >= chunks)
        def _():
            ch = step + 1 - chunks
            wait_bytes(behind.at[0, ch], halo_recv.at[ch])

        conv = invert(parts[0], parts[1])
        tile_ends(step - 1, (0,))
        finish_tile(step, conv)
        begun = begin_tile(step + 1)
        tile_ends(step - 1, (1,))
        keep_parts(begun)

        @pl.when(step - 1 >= chunks)
        def _():
            send_ends(step - 1 - chunks)

        return carry

    lax.fori_loop(0, chunks, tap_chunk, 0)
    last = 2 * chunks - 1
    keep_parts(begin_tile(0))
    first_conv = invert(parts[0], parts[1])
    keep_parts(begin_tile(1))
    finish_tile(0, first_conv)
    lax.fori_loop(1, last, forward_step, 0)
    last_conv = invert(parts[0], parts[1])
    tile_ends(last - 1, (0, 1))
    finish_tile(last, last_conv)
    send_ends(chunks - 2)
    tile_ends(last, (0, 1))
    send_ends(chunks - 1)
    pltpu.make_async_copy(esend.at[me], erecv.at[me], e_recv).start()

    def inside_chunk(ch, carry):
        start = pl.multiple_of(ch * WIDE, WIDE)
        highs, lows = [], []
        for group in range(2):
            lanes = pl.ds(start + group * LANES, LANES)
            power_of = [amp[m : m + 1, lanes] * zb[m, :, lanes] for m in range(MODES)]
            steps = [z8[m : m + 1, lanes] for m in range(MODES)]
            pieces = []
            for block in range(TILE // 8):
                total = power_of[0]
                for p in power_of[1:]:
                    total = total + p
                pieces.append(total)
                if block < TILE // 8 - 1:
                    power_of = [p * z for p, z in zip(power_of, steps)]
            lag_taps = jnp.concatenate(pieces, axis=0)
            high = lag_taps.astype(jnp.bfloat16)
            highs.append(high)
            lows.append((lag_taps - high.astype(jnp.float32)).astype(jnp.bfloat16))
        high = jnp.concatenate(highs, axis=1)
        low = jnp.concatenate(lows, axis=1)
        stacked = jnp.concatenate([high, high, low], axis=0)
        spectrum = jnp.dot(ahead[...], stacked, preferred_element_type=jnp.float32)
        for half in range(2):
            inside[half, ch] = convolve(transform(longin[half, ch]), spectrum)
        return carry

    lax.fori_loop(0, chunks // 2, inside_chunk, 0)

    wait_bytes(erecv, e_recv)
    my_cols = pl.ds(pl.multiple_of((me // 2) * LANES, LANES), LANES)
    my_rate = rate[pl.ds(pl.multiple_of(8 * lax.rem(me, 2), 8), 8), my_cols]
    block_decay = jnp.exp(-2.0 * TILE * my_rate)

    def scan_step(n, state):
        ssend[n] = state
        through = flag(jnp.logical_and(n > 0, docs[jnp.maximum(2 * n - 1, 0)] == docs[2 * n + 1]))
        return (block_decay * through) * state + erecv[n]

    lax.fori_loop(0, seq_count, scan_step, jnp.zeros((8, LANES), jnp.float32))

    slot = me // 4

    def hand_back(step, carry):
        target = lax.rem(me + step, seq_count)
        pltpu.make_async_remote_copy(
            src_ref=ssend.at[target], dst_ref=srecv.at[me], send_sem=s_send, recv_sem=s_recv.at[slot],
            device_id=(target, part), device_id_type=MESH).start()
        return carry

    lax.fori_loop(1, seq_count, hand_back, 0)
    pltpu.make_async_copy(ssend.at[me], srecv.at[me], s_recv.at[slot]).start()

    lax.fori_loop(chunks // 2, chunks, inside_chunk, 0)

    power[...] = jnp.zeros_like(power)

    def outward_chunk(ch, carry):
        start = pl.multiple_of(ch * WIDE, WIDE)
        tiles = pl.ds(pl.multiple_of(4 * ch, 4), 4)
        wait_bytes(srecv.at[tiles], s_recv.at[ch])
        for group in range(2):
            lanes = pl.ds(start + group * LANES, LANES)
            steps = [z8[m : m + 1, lanes] for m in range(MODES)]
            states = [kept0 * srecv[4 * ch + 2 * group + n] for n in range(2)]
            for half in range(2):
                if half == 1:
                    states = [
                        kept1 * (z128[8 * n : 8 * n + 8, lanes] * s + ends[0, 8 * n : 8 * n + 8, lanes])
                        for n, s in enumerate(states)
                    ]
                begun = [amp[8 * n : 8 * n + 8, lanes] * z1[8 * n : 8 * n + 8, lanes] * s for n, s in enumerate(states)]
                waves = [begun[m // 8][m % 8 : m % 8 + 1] * zb[m, :, lanes] for m in range(MODES)]
                for block in range(TILE // 8):
                    total = inside[half, ch, 8 * block : 8 * block + 8, group * LANES : (group + 1) * LANES]
                    for w in waves:
                        total = total + w
                    rows = pl.ds(half * TILE + 8 * block, 8)
                    total = total * q2[rows, lanes].astype(jnp.float32)
                    longout[rows, lanes] = total
                    power[rows, :] = power[rows, :] + total * total
                    if block < TILE // 8 - 1:
                        waves = [w * z for w, z in zip(waves, steps)]
        return carry

    lax.fori_loop(0, chunks, outward_chunk, 0)

    psend[...] = jnp.zeros_like(psend)
    for half in range(2):
        turned = power[half * TILE : (half + 1) * TILE, :].T
        psend[half : half + 1, :] = jnp.sum(turned, axis=0, keepdims=True)
    for step in range(1, mp_count):
        pltpu.make_async_remote_copy(
            src_ref=psend, dst_ref=precv.at[part], send_sem=p_send, recv_sem=p_recv,
            device_id=(me, lax.rem(part + step, mp_count)), device_id_type=MESH).start()
    precv[part] = psend[...]
    others = pl.ds(0, mp_count - 1)
    wait_bytes(precv.at[others], p_recv)
    total = precv[0]
    for n in range(1, mp_count):
        total = total + precv[n]
    scale = lax.rsqrt(total / (channels * mp_count) + norm_eps)
    for half in range(2):
        column = jnp.broadcast_to(scale[half : half + 1, :], (TILE, LANES)).T
        rows = pl.ds(half * TILE, TILE)
        for group in range(channels // LANES):
            lanes = slice(group * LANES, (group + 1) * LANES)
            outbuf[rows, lanes] = (longout[rows, lanes] * column).astype(jnp.bfloat16)

    wait_bytes(outgoing, halo_send)
    wait_bytes(esend.at[pl.ds(0, seq_count - 1)], e_send)
    wait_bytes(ssend.at[pl.ds(0, seq_count - 1)], s_send)
    wait_bytes(precv.at[others], p_send)


def on_device(mesh_sizes, values, k_first, q_first, k_second, q_second, mr_taps, li_rate, li_residue, tile_docs):
    seq_count, mp_count = mesh_sizes
    rows, channels = values.shape
    chunks = channels // WIDE
    ahead, pair, back = dft_tables()
    f32, bf16 = jnp.float32, jnp.bfloat16
    vmem = pltpu.VMEM
    hbm_spec = pl.BlockSpec(memory_space=pltpu.MemorySpace.HBM)
    big = vmem((rows, channels), bf16)
    modal = vmem((MODES, channels), f32)
    tiles = vmem((seq_count, 8, LANES), f32)
    dma = pltpu.SemaphoreType.DMA
    return pl.pallas_call(
        functools.partial(kernel, seq_count, mp_count),
        out_shape=vmem((rows, channels), bf16),
        in_specs=[pl.BlockSpec(memory_space=pltpu.SMEM)] + [hbm_spec] * 11,
        out_specs=pl.BlockSpec(memory_space=pltpu.VMEM),
        scratch_shapes=[
            big, big, big, big, big,
            vmem((TILE, channels), bf16),
            modal, modal,
            vmem(ahead.shape, bf16),
            vmem(pair.shape, bf16),
            vmem(back.shape, bf16),
            vmem((2, chunks, TILE, WIDE), bf16),
            vmem((2, chunks, TILE, WIDE), bf16),
            vmem((chunks, TILE, WIDE), bf16),
            vmem((2, chunks, TILE, WIDE), bf16),
            vmem((2, chunks, TILE, WIDE), f32),
            vmem((rows, channels), f32),
            modal, modal, modal, modal,
            vmem((MODES, 8, channels), f32),
            vmem((MODES, 8, channels), f32),
            vmem((chunks, 2 * TILE, WIDE), f32),
            vmem((2, 2 * TILE, WIDE), bf16),
            vmem((2, MODES, channels), f32),
            tiles, tiles, tiles, tiles,
            vmem((rows, LANES), f32),
            vmem((8, LANES), f32),
            vmem((mp_count, 8, LANES), f32),
            dma((2, chunks)),
            dma((9,)),
            dma,
            dma((chunks,)),
            dma, dma, dma,
            dma((chunks,)),
            dma, dma,
        ],
        compiler_params=pltpu.CompilerParams(
            collective_id=0, has_side_effects=True, vmem_limit_bytes=56 * 1024 * 1024),
    )(tile_docs, values, k_first, q_first, k_second, q_second, mr_taps, li_rate, li_residue,
      jnp.asarray(ahead), jnp.asarray(pair), jnp.asarray(back))


def solution(mesh):
    sizes = (mesh.shape["seq"], mesh.shape["mp"])
    block = P("seq", "mp")
    param = P(None, "mp")
    return jax.shard_map(
        functools.partial(on_device, sizes),
        mesh=mesh,
        in_specs=(block, block, block, block, block, param, param, param, P()),
        out_specs=block,
        check_vma=False,
    )
```

```python
import functools
import jax
import jax.numpy as jnp
import numpy as np
from jax import lax
from jax.experimental import pallas as pl
from jax.experimental.pallas import tpu as pltpu
from jax.sharding import PartitionSpec as P

TILE = 128
MODES = 16
LANES = 128
WIDE = 256
norm_eps = 1e-06
MESH = pl.DeviceIdType.MESH


def split_bf16(table):
    high = table.astype(jnp.bfloat16)
    low = (table - high.astype(np.float64)).astype(jnp.bfloat16)
    return np.asarray(high), np.asarray(low)


def dft_tables():
    freq = 2.0 * np.pi * (4.0 * np.arange(TILE) + 1.0) / (4.0 * TILE)
    angle = freq[:, None] * np.arange(TILE)[None, :]
    real, imag = np.cos(angle), -np.sin(angle)

    def mixed(top, bottom):
        blocks = [part.reshape(TILE // 16, 1, 16, TILE) for part in (top, bottom)]
        return np.concatenate(blocks, axis=1).reshape(2 * TILE, TILE)

    current = mixed(real, imag)
    c_high, c_low = split_bf16(current)
    p_high, p_low = split_bf16(mixed(-imag, real))
    g_high, g_low = split_bf16(current.T / TILE)
    ahead = np.concatenate([c_high, c_low, c_high], axis=1)
    pair = np.concatenate([c_high, p_high, c_low, p_low], axis=1)
    back = np.concatenate([g_high, g_low], axis=0)
    return ahead, pair, back


def wait_bytes(ref, sem):
    pltpu.make_async_copy(ref, ref, sem).wait()


def parts_of(spectrum):
    blocks = spectrum.reshape(TILE // 16, 2, 16, WIDE)
    return blocks[:, 0], blocks[:, 1]


def woven(real, imag):
    return jnp.stack([real, imag], axis=1).reshape(2 * TILE, WIDE)


def kernel(
    seq_count, mp_count,
    docs, values_h, k1_h, q1_h, k2_h, q2_h, taps_h, rate_h, resid_h, ahead_h, pair_h, back_h,
    outbuf,
    values, k1, q1, k2, q2, taps, rate, resid, ahead, pair, back,
    gated, behind, outgoing, longin, inside, longout, amp, z1, z8, z128, zb, zr,
    spectra, parts, ends, esend, erecv, ssend, srecv, power, psend, precv,
    in_sem, par_sem, halo_send, halo_recv, e_send, e_recv, s_send, s_recv, p_send, p_recv,
):
    me = lax.axis_index("seq")
    part = lax.axis_index("mp")
    channels = values.shape[1]
    chunks = channels // WIDE

    def in_copy(source, target, row, ch):
        cols = pl.ds(ch * WIDE, WIDE)
        return pltpu.make_async_copy(source.at[:, cols], target.at[:, cols], in_sem.at[row, ch])

    for ch in range(chunks):
        in_copy(values_h, values, 0, ch).start()
        in_copy(k1_h, k1, 1, ch).start()

    barrier = pltpu.get_barrier_semaphore()

    def greet(step, carry):
        pl.semaphore_signal(barrier, inc=1, device_id=(lax.rem(me + step, seq_count), part), device_id_type=MESH)
        return carry

    lax.fori_loop(1, seq_count, greet, 0)
    for step in range(1, mp_count):
        pl.semaphore_signal(barrier, inc=1, device_id=(me, lax.rem(part + step, mp_count)), device_id_type=MESH)

    whole = [(rate_h, rate), (resid_h, resid), (taps_h, taps), (ahead_h, ahead), (pair_h, pair), (back_h, back),
             (q1_h, q1), (k2_h, k2), (q2_h, q2)]
    whole_copies = [pltpu.make_async_copy(a, b, par_sem.at[n]) for n, (a, b) in enumerate(whole)]
    for copy in whole_copies:
        copy.start()

    first = 2 * me
    doc_a = docs[first]
    doc_b = docs[first + 1]

    def flag(test):
        return jnp.where(test, 1.0, 0.0).astype(jnp.float32)

    kept0 = flag(jnp.logical_and(me > 0, docs[jnp.maximum(first - 1, 0)] == doc_a))
    kept1 = flag(doc_a == doc_b)
    doc_after = docs[jnp.minimum(first + 2, 2 * seq_count - 1)]
    kept2 = flag(jnp.logical_and(me < seq_count - 1, doc_after == doc_b))

    for ch in range(chunks):
        in_copy(values_h, values, 0, ch).wait()
        in_copy(k1_h, k1, 1, ch).wait()
        cols = pl.ds(ch * WIDE, WIDE)
        rows = pl.ds(TILE, TILE)
        product = k1[rows, cols].astype(jnp.float32) * values[rows, cols].astype(jnp.float32)
        gated[1, ch] = product.astype(jnp.bfloat16)
        outgoing[ch] = (kept2 * product).astype(jnp.bfloat16)

    pl.semaphore_wait(barrier, seq_count - 1 + mp_count - 1)
    after = lax.rem(me + 1, seq_count)

    for ch in range(chunks):
        pltpu.make_async_remote_copy(
            src_ref=outgoing.at[ch], dst_ref=behind.at[0, ch], send_sem=halo_send, recv_sem=halo_recv.at[ch],
            device_id=(after, part), device_id_type=MESH).start()

    for ch in range(chunks):
        cols = pl.ds(ch * WIDE, WIDE)
        rows = pl.ds(0, TILE)
        product = k1[rows, cols].astype(jnp.float32) * values[rows, cols].astype(jnp.float32)
        gated[0, ch] = product.astype(jnp.bfloat16)
        behind[1, ch] = (kept1 * product).astype(jnp.bfloat16)

    for copy in whole_copies[:2]:
        copy.wait()
    r_all = rate[...]
    z8[...] = jnp.exp(-8.0 * r_all)
    z128[...] = jnp.exp(-float(TILE) * r_all)
    sub = lax.broadcasted_iota(jnp.int32, (8, WIDE), 0).astype(jnp.float32)

    def fill_zr(ch, carry):
        cols = pl.ds(pl.multiple_of(ch * WIDE, WIDE), WIDE)
        for m in range(MODES):
            zr[m, :, cols] = jnp.exp(-rate[m : m + 1, cols] * (7.0 - sub))
        return carry

    lax.fori_loop(0, chunks, fill_zr, 0)

    for copy in whole_copies[2:]:
        copy.wait()

    def transform(tile):
        doubled = jnp.concatenate([tile, tile], axis=0)
        return jnp.dot(ahead[:, : 2 * TILE], doubled, preferred_element_type=jnp.float32)

    def product_of(spectrum, filter_spectrum):
        real, imag = parts_of(spectrum)
        s_real, s_imag = parts_of(filter_spectrum)
        product = woven(real * s_real - imag * s_imag, real * s_imag + imag * s_real)
        high = product.astype(jnp.bfloat16)
        low = (product - high.astype(jnp.float32)).astype(jnp.bfloat16)
        return high, low

    def invert(high, low):
        both = jnp.dot(back[...], high, preferred_element_type=jnp.float32)
        fine = jnp.dot(back[:TILE], low, preferred_element_type=jnp.float32)
        return both[:TILE] + (both[TILE:] + fine)

    def convolve(spectrum, filter_spectrum):
        return invert(*product_of(spectrum, filter_spectrum))

    def place_of(step):
        half = 1 - step // chunks
        ch = lax.rem(step, chunks)
        return half, ch, pl.multiple_of(ch * WIDE, WIDE)

    def begin_tile(step):
        half, ch, start = place_of(step)
        current, previous = gated[half, ch], behind[half, ch]
        stacked = jnp.concatenate([current, previous, current, previous], axis=0)
        spectrum = jnp.dot(pair[...], stacked, preferred_element_type=jnp.float32)
        return spectrum, spectra[ch]

    def keep_parts(begun):
        parts[0], parts[1] = product_of(*begun)

    def finish_tile(step, conv):
        half, ch, start = place_of(step)
        cols = pl.ds(start, WIDE)
        rows = pl.ds(pl.multiple_of(half * TILE, TILE), TILE)
        short = (q1[rows, cols].astype(jnp.float32) * conv).astype(jnp.bfloat16)
        longin[half, ch] = (k2[rows, cols].astype(jnp.float32) * short.astype(jnp.float32)).astype(jnp.bfloat16)

    def tile_ends(step, groups):
        half, ch, start = place_of(step)
        for group in groups:
            lanes = pl.ds(start + group * LANES, LANES)
            tile = longin[half, ch, :, group * LANES : (group + 1) * LANES].astype(jnp.float32)
            steps = [z8[m : m + 1, lanes] for m in range(MODES)]
            sums = [tile[0:8]] * MODES
            for block in range(1, TILE // 8):
                row = tile[8 * block : 8 * block + 8]
                sums = [s * z + row for s, z in zip(sums, steps)]
            for m, s in enumerate(sums):
                ends[half, m : m + 1, lanes] = jnp.sum(s * zr[m, :, lanes], axis=0, keepdims=True)

    def tap_chunk(ch, carry):
        spectra[ch] = transform(taps[:, pl.ds(pl.multiple_of(ch * WIDE, WIDE), WIDE)])
        return carry

    def send_ends(ch):
        for piece in range(4):
            owner = 4 * ch + piece
            lanes = pl.ds(pl.multiple_of(ch * WIDE, WIDE) + (piece // 2) * LANES, LANES)
            modes = pl.ds(8 * (piece % 2), 8)
            esend[owner] = ends[1, modes, lanes] + kept1 * z128[modes, lanes] * ends[0, modes, lanes]
        for piece in range(4):
            owner = 4 * ch + piece

            @pl.when(owner != me)
            def _():
                pltpu.make_async_remote_copy(
                    src_ref=esend.at[owner], dst_ref=erecv.at[me], send_sem=e_send, recv_sem=e_recv,
                    device_id=(owner, part), device_id_type=MESH).start()

    def forward_step(step, carry):
        @pl.when(step + 1 >= chunks)
        def _():
            ch = step + 1 - chunks
            wait_bytes(behind.at[0, ch], halo_recv.at[ch])

        tile_ends(step - 1, (0, 1))
        conv = invert(parts[0], parts[1])
        begun = begin_tile(step + 1)
        finish_tile(step, conv)
        keep_parts(begun)

        @pl.when(step - 1 >= chunks)
        def _():
            send_ends(step - 1 - chunks)

        return carry

    lax.fori_loop(0, chunks, tap_chunk, 0)
    last = 2 * chunks - 1
    keep_parts(begin_tile(0))
    first_conv = invert(parts[0], parts[1])
    keep_parts(begin_tile(1))
    finish_tile(0, first_conv)
    lax.fori_loop(1, last, forward_step, 0)
    last_conv = invert(parts[0], parts[1])
    tile_ends(last - 1, (0, 1))
    finish_tile(last, last_conv)
    send_ends(chunks - 2)
    tile_ends(last, (0, 1))
    send_ends(chunks - 1)
    pltpu.make_async_copy(esend.at[me], erecv.at[me], e_recv).start()

    amp[...] = resid[...] * jnp.sqrt(rate[...])
    z1[...] = jnp.exp(-rate[...])

    def inside_chunk(ch):
        start = pl.multiple_of(ch * WIDE, WIDE)
        cols = pl.ds(start, WIDE)
        for m in range(MODES):
            zb[m, :, cols] = jnp.exp(-rate[m : m + 1, cols] * sub)
        highs, lows = [], []
        for group in range(2):
            lanes = pl.ds(start + group * LANES, LANES)
            power_of = [amp[m : m + 1, lanes] * zb[m, :, lanes] for m in range(MODES)]
            steps = [z8[m : m + 1, lanes] for m in range(MODES)]
            pieces = []
            for block in range(TILE // 8):
                total = power_of[0]
                for p in power_of[1:]:
                    total = total + p
                pieces.append(total)
                if block < TILE // 8 - 1:
                    power_of = [p * z for p, z in zip(power_of, steps)]
            lag_taps = jnp.concatenate(pieces, axis=0)
            high = lag_taps.astype(jnp.bfloat16)
            highs.append(high)
            lows.append((lag_taps - high.astype(jnp.float32)).astype(jnp.bfloat16))
        high = jnp.concatenate(highs, axis=1)
        low = jnp.concatenate(lows, axis=1)
        stacked = jnp.concatenate([high, high, low], axis=0)
        spectrum = jnp.dot(ahead[...], stacked, preferred_element_type=jnp.float32)
        for half in range(2):
            inside[half, ch] = convolve(transform(longin[half, ch]), spectrum)

    my_cols = pl.ds(pl.multiple_of((me // 2) * LANES, LANES), LANES)
    my_rate = rate[pl.ds(pl.multiple_of(8 * lax.rem(me, 2), 8), 8), my_cols]
    block_decay = jnp.exp(-2.0 * TILE * my_rate)
    slot = me // 4

    def scan_step(n, state):
        ssend[n] = state
        through = flag(jnp.logical_and(n > 0, docs[jnp.maximum(2 * n - 1, 0)] == docs[2 * n + 1]))
        return (block_decay * through) * state + erecv[n]

    def hand_back(step, carry):
        target = lax.rem(me + step, seq_count)
        pltpu.make_async_remote_copy(
            src_ref=ssend.at[target], dst_ref=srecv.at[me], send_sem=s_send, recv_sem=s_recv.at[slot],
            device_id=(target, part), device_id_type=MESH).start()
        return carry

    def middle_chunk(ch, carry):
        @pl.when(ch == 2 + slot // 2)
        def _():
            wait_bytes(erecv, e_recv)
            lax.fori_loop(0, seq_count, scan_step, jnp.zeros((8, LANES), jnp.float32), unroll=8)
            lax.fori_loop(1, seq_count, hand_back, 0)
            pltpu.make_async_copy(ssend.at[me], srecv.at[me], s_recv.at[slot]).start()

        inside_chunk(ch)
        return carry

    lax.fori_loop(0, chunks, middle_chunk, 0)

    power[...] = jnp.zeros_like(power)

    def outward_chunk(ch, carry):
        start = pl.multiple_of(ch * WIDE, WIDE)
        tiles = pl.ds(pl.multiple_of(4 * ch, 4), 4)
        wait_bytes(srecv.at[tiles], s_recv.at[ch])
        for group in range(2):
            lanes = pl.ds(start + group * LANES, LANES)
            steps = [z8[m : m + 1, lanes] for m in range(MODES)]
            states = [kept0 * srecv[4 * ch + 2 * group + n] for n in range(2)]
            for half in range(2):
                if half == 1:
                    states = [
                        kept1 * (z128[8 * n : 8 * n + 8, lanes] * s + ends[0, 8 * n : 8 * n + 8, lanes])
                        for n, s in enumerate(states)
                    ]
                begun = [amp[8 * n : 8 * n + 8, lanes] * z1[8 * n : 8 * n + 8, lanes] * s for n, s in enumerate(states)]
                waves = [begun[m // 8][m % 8 : m % 8 + 1] * zb[m, :, lanes] for m in range(MODES)]
                for block in range(TILE // 8):
                    total = inside[half, ch, 8 * block : 8 * block + 8, group * LANES : (group + 1) * LANES]
                    for w in waves:
                        total = total + w
                    rows = pl.ds(half * TILE + 8 * block, 8)
                    total = total * q2[rows, lanes].astype(jnp.float32)
                    longout[rows, lanes] = total
                    power[rows, :] = power[rows, :] + total * total
                    if block < TILE // 8 - 1:
                        waves = [w * z for w, z in zip(waves, steps)]
        return carry

    lax.fori_loop(0, chunks, outward_chunk, 0)

    psend[...] = jnp.zeros_like(psend)
    for half in range(2):
        turned = power[half * TILE : (half + 1) * TILE, :].T
        psend[half : half + 1, :] = jnp.sum(turned, axis=0, keepdims=True)
    for step in range(1, mp_count):
        pltpu.make_async_remote_copy(
            src_ref=psend, dst_ref=precv.at[part], send_sem=p_send, recv_sem=p_recv,
            device_id=(me, lax.rem(part + step, mp_count)), device_id_type=MESH).start()
    precv[part] = psend[...]
    others = pl.ds(0, mp_count - 1)
    wait_bytes(precv.at[others], p_recv)
    total = precv[0]
    for n in range(1, mp_count):
        total = total + precv[n]
    scale = lax.rsqrt(total / (channels * mp_count) + norm_eps)
    for half in range(2):
        column = jnp.broadcast_to(scale[half : half + 1, :], (TILE, LANES)).T
        rows = pl.ds(half * TILE, TILE)
        for group in range(channels // LANES):
            lanes = slice(group * LANES, (group + 1) * LANES)
            outbuf[rows, lanes] = (longout[rows, lanes] * column).astype(jnp.bfloat16)

    wait_bytes(outgoing, halo_send)
    wait_bytes(esend.at[pl.ds(0, seq_count - 1)], e_send)
    wait_bytes(ssend.at[pl.ds(0, seq_count - 1)], s_send)
    wait_bytes(precv.at[others], p_send)


def on_device(mesh_sizes, values, k_first, q_first, k_second, q_second, mr_taps, li_rate, li_residue, tile_docs):
    seq_count, mp_count = mesh_sizes
    rows, channels = values.shape
    chunks = channels // WIDE
    ahead, pair, back = dft_tables()
    f32, bf16 = jnp.float32, jnp.bfloat16
    vmem = pltpu.VMEM
    hbm_spec = pl.BlockSpec(memory_space=pltpu.MemorySpace.HBM)
    big = vmem((rows, channels), bf16)
    modal = vmem((MODES, channels), f32)
    tiles = vmem((seq_count, 8, LANES), f32)
    dma = pltpu.SemaphoreType.DMA
    return pl.pallas_call(
        functools.partial(kernel, seq_count, mp_count),
        out_shape=vmem((rows, channels), bf16),
        in_specs=[pl.BlockSpec(memory_space=pltpu.SMEM)] + [hbm_spec] * 11,
        out_specs=pl.BlockSpec(memory_space=pltpu.VMEM),
        scratch_shapes=[
            big, big, big, big, big,
            vmem((TILE, channels), bf16),
            modal, modal,
            vmem(ahead.shape, bf16),
            vmem(pair.shape, bf16),
            vmem(back.shape, bf16),
            vmem((2, chunks, TILE, WIDE), bf16),
            vmem((2, chunks, TILE, WIDE), bf16),
            vmem((chunks, TILE, WIDE), bf16),
            vmem((2, chunks, TILE, WIDE), bf16),
            vmem((2, chunks, TILE, WIDE), f32),
            vmem((rows, channels), f32),
            modal, modal, modal, modal,
            vmem((MODES, 8, channels), f32),
            vmem((MODES, 8, channels), f32),
            vmem((chunks, 2 * TILE, WIDE), f32),
            vmem((2, 2 * TILE, WIDE), bf16),
            vmem((2, MODES, channels), f32),
            tiles, tiles, tiles, tiles,
            vmem((rows, LANES), f32),
            vmem((8, LANES), f32),
            vmem((mp_count, 8, LANES), f32),
            dma((2, chunks)),
            dma((9,)),
            dma,
            dma((chunks,)),
            dma, dma, dma,
            dma((chunks,)),
            dma, dma,
        ],
        compiler_params=pltpu.CompilerParams(
            collective_id=0, has_side_effects=True, vmem_limit_bytes=56 * 1024 * 1024),
    )(tile_docs, values, k_first, q_first, k_second, q_second, mr_taps, li_rate, li_residue,
      jnp.asarray(ahead), jnp.asarray(pair), jnp.asarray(back))


def solution(mesh):
    sizes = (mesh.shape["seq"], mesh.shape["mp"])
    block = P("seq", "mp")
    param = P(None, "mp")
    return jax.shard_map(
        functools.partial(on_device, sizes),
        mesh=mesh,
        in_specs=(block, block, block, block, block, param, param, param, P()),
        out_specs=block,
        check_vma=False,
    )
```

```python
import functools
import jax
import jax.numpy as jnp
import numpy as np
from jax import lax
from jax.experimental import pallas as pl
from jax.experimental.pallas import tpu as pltpu
from jax.sharding import PartitionSpec as P

TILE = 128
MODES = 16
LANES = 128
WIDE = 256
norm_eps = 1e-06
MESH = pl.DeviceIdType.MESH


def split_bf16(table):
    high = table.astype(jnp.bfloat16)
    low = (table - high.astype(np.float64)).astype(jnp.bfloat16)
    return np.asarray(high), np.asarray(low)


def dft_tables():
    freq = 2.0 * np.pi * (4.0 * np.arange(TILE) + 1.0) / (4.0 * TILE)
    angle = freq[:, None] * np.arange(TILE)[None, :]
    real, imag = np.cos(angle), -np.sin(angle)

    def mixed(top, bottom):
        blocks = [part.reshape(TILE // 16, 1, 16, TILE) for part in (top, bottom)]
        return np.concatenate(blocks, axis=1).reshape(2 * TILE, TILE)

    current = mixed(real, imag)
    c_high, c_low = split_bf16(current)
    p_high, p_low = split_bf16(mixed(-imag, real))
    g_high, g_low = split_bf16(current.T / TILE)
    ahead = np.concatenate([c_high, c_low, c_high], axis=1)
    pair = np.concatenate([c_high, p_high, c_low, p_low], axis=1)
    back = np.concatenate([g_high, g_low], axis=0)
    return ahead, pair, back


def wait_bytes(ref, sem):
    pltpu.make_async_copy(ref, ref, sem).wait()


def parts_of(spectrum):
    blocks = spectrum.reshape(TILE // 16, 2, 16, WIDE)
    return blocks[:, 0], blocks[:, 1]


def woven(real, imag):
    return jnp.stack([real, imag], axis=1).reshape(2 * TILE, WIDE)


def kernel(
    seq_count, mp_count,
    docs, values_h, k1_h, q1_h, k2_h, q2_h, taps_h, rate_h, resid_h, ahead_h, pair_h, back_h,
    outbuf,
    values, k1, q1, k2, q2, taps, rate, resid, ahead, pair, back,
    gated, behind, outgoing, longin, inside, longout, amp, z1, z8, z128, zb, zr,
    spectra, parts, lag, ends, esend, erecv, ssend, srecv, power, psend, precv,
    in_sem, par_sem, halo_send, halo_recv, e_send, e_recv, s_send, s_recv, p_send, p_recv,
):
    me = lax.axis_index("seq")
    part = lax.axis_index("mp")
    channels = values.shape[1]
    chunks = channels // WIDE

    def in_copy(source, target, row, ch):
        cols = pl.ds(ch * WIDE, WIDE)
        return pltpu.make_async_copy(source.at[:, cols], target.at[:, cols], in_sem.at[row, ch])

    whole = [(rate_h, rate), (resid_h, resid), (taps_h, taps), (ahead_h, ahead), (pair_h, pair), (back_h, back),
             (q1_h, q1), (k2_h, k2), (q2_h, q2)]
    whole_copies = [pltpu.make_async_copy(a, b, par_sem.at[n]) for n, (a, b) in enumerate(whole)]
    whole_copies[0].start()
    for ch in range(chunks):
        in_copy(values_h, values, 0, ch).start()
        in_copy(k1_h, k1, 1, ch).start()

    barrier = pltpu.get_barrier_semaphore()

    def greet(step, carry):
        pl.semaphore_signal(barrier, inc=1, device_id=(lax.rem(me + step, seq_count), part), device_id_type=MESH)
        return carry

    lax.fori_loop(1, seq_count, greet, 0)
    for step in range(1, mp_count):
        pl.semaphore_signal(barrier, inc=1, device_id=(me, lax.rem(part + step, mp_count)), device_id_type=MESH)

    for copy in whole_copies[1:]:
        copy.start()

    first = 2 * me
    doc_a = docs[first]
    doc_b = docs[first + 1]

    def flag(test):
        return jnp.where(test, 1.0, 0.0).astype(jnp.float32)

    kept0 = flag(jnp.logical_and(me > 0, docs[jnp.maximum(first - 1, 0)] == doc_a))
    kept1 = flag(doc_a == doc_b)
    doc_after = docs[jnp.minimum(first + 2, 2 * seq_count - 1)]
    kept2 = flag(jnp.logical_and(me < seq_count - 1, doc_after == doc_b))

    whole_copies[0].wait()
    r_all = rate[...]
    z8[...] = jnp.exp(-8.0 * r_all)
    z128[...] = jnp.exp(-float(TILE) * r_all)
    sub = lax.broadcasted_iota(jnp.int32, (8, WIDE), 0).astype(jnp.float32)

    def fill_zr(ch, carry):
        cols = pl.ds(pl.multiple_of(ch * WIDE, WIDE), WIDE)
        for m in range(MODES):
            zr[m, :, cols] = jnp.exp(-rate[m : m + 1, cols] * (7.0 - sub))
        return carry

    lax.fori_loop(0, chunks, fill_zr, 0)

    for ch in range(chunks):
        in_copy(values_h, values, 0, ch).wait()
        in_copy(k1_h, k1, 1, ch).wait()
        cols = pl.ds(ch * WIDE, WIDE)
        rows = pl.ds(TILE, TILE)
        product = k1[rows, cols].astype(jnp.float32) * values[rows, cols].astype(jnp.float32)
        gated[1, ch] = product.astype(jnp.bfloat16)
        outgoing[ch] = (kept2 * product).astype(jnp.bfloat16)

    pl.semaphore_wait(barrier, seq_count - 1 + mp_count - 1)
    after = lax.rem(me + 1, seq_count)

    for ch in range(chunks):
        pltpu.make_async_remote_copy(
            src_ref=outgoing.at[ch], dst_ref=behind.at[0, ch], send_sem=halo_send, recv_sem=halo_recv.at[ch],
            device_id=(after, part), device_id_type=MESH).start()

    for ch in range(chunks):
        cols = pl.ds(ch * WIDE, WIDE)
        rows = pl.ds(0, TILE)
        product = k1[rows, cols].astype(jnp.float32) * values[rows, cols].astype(jnp.float32)
        gated[0, ch] = product.astype(jnp.bfloat16)
        behind[1, ch] = (kept1 * product).astype(jnp.bfloat16)

    for copy in whole_copies[1:]:
        copy.wait()

    def transform(tile):
        doubled = jnp.concatenate([tile, tile], axis=0)
        return jnp.dot(ahead[:, : 2 * TILE], doubled, preferred_element_type=jnp.float32)

    def product_of(spectrum, filter_spectrum):
        real, imag = parts_of(spectrum)
        s_real, s_imag = parts_of(filter_spectrum)
        product = woven(real * s_real - imag * s_imag, real * s_imag + imag * s_real)
        high = product.astype(jnp.bfloat16)
        low = (product - high.astype(jnp.float32)).astype(jnp.bfloat16)
        return high, low

    def invert(high, low):
        both = jnp.dot(back[...], high, preferred_element_type=jnp.float32)
        fine = jnp.dot(back[:TILE], low, preferred_element_type=jnp.float32)
        return both[:TILE] + (both[TILE:] + fine)

    def convolve(spectrum, filter_spectrum):
        return invert(*product_of(spectrum, filter_spectrum))

    def place_of(step):
        half = 1 - step // chunks
        ch = lax.rem(step, chunks)
        return half, ch, pl.multiple_of(ch * WIDE, WIDE)

    def begin_tile(step):
        half, ch, start = place_of(step)
        current, previous = gated[half, ch], behind[half, ch]
        stacked = jnp.concatenate([current, previous, current, previous], axis=0)
        spectrum = jnp.dot(pair[...], stacked, preferred_element_type=jnp.float32)
        return spectrum, spectra[ch]

    def keep_parts(begun):
        parts[0], parts[1] = product_of(*begun)

    def finish_tile(step, conv):
        half, ch, start = place_of(step)
        cols = pl.ds(start, WIDE)
        rows = pl.ds(pl.multiple_of(half * TILE, TILE), TILE)
        short = (q1[rows, cols].astype(jnp.float32) * conv).astype(jnp.bfloat16)
        longin[half, ch] = (k2[rows, cols].astype(jnp.float32) * short.astype(jnp.float32)).astype(jnp.bfloat16)

    def tile_ends(step, groups):
        half, ch, start = place_of(step)
        for group in groups:
            lanes = pl.ds(start + group * LANES, LANES)
            tile = longin[half, ch, :, group * LANES : (group + 1) * LANES].astype(jnp.float32)
            steps = [z8[m : m + 1, lanes] for m in range(MODES)]
            sums = [tile[0:8]] * MODES
            for block in range(1, TILE // 8):
                row = tile[8 * block : 8 * block + 8]
                sums = [s * z + row for s, z in zip(sums, steps)]
            for m, s in enumerate(sums):
                ends[half, m : m + 1, lanes] = jnp.sum(s * zr[m, :, lanes], axis=0, keepdims=True)

    def tap_chunk(ch, carry):
        spectra[ch] = transform(taps[:, pl.ds(pl.multiple_of(ch * WIDE, WIDE), WIDE)])
        return carry

    def send_ends(ch):
        for piece in range(4):
            owner = 4 * ch + piece
            lanes = pl.ds(pl.multiple_of(ch * WIDE, WIDE) + (piece // 2) * LANES, LANES)
            modes = pl.ds(8 * (piece % 2), 8)
            esend[owner] = ends[1, modes, lanes] + kept1 * z128[modes, lanes] * ends[0, modes, lanes]
        for piece in range(4):
            owner = 4 * ch + piece

            @pl.when(owner != me)
            def _():
                pltpu.make_async_remote_copy(
                    src_ref=esend.at[owner], dst_ref=erecv.at[me], send_sem=e_send, recv_sem=e_recv,
                    device_id=(owner, part), device_id_type=MESH).start()

    def forward_step(step, carry):
        @pl.when(step + 1 >= chunks)
        def _():
            ch = step + 1 - chunks
            wait_bytes(behind.at[0, ch], halo_recv.at[ch])

        tile_ends(step - 1, (0, 1))
        conv = invert(parts[0], parts[1])
        begun = begin_tile(step + 1)
        finish_tile(step, conv)
        keep_parts(begun)

        @pl.when(step - 1 >= chunks)
        def _():
            send_ends(step - 1 - chunks)

        return carry

    lax.fori_loop(0, chunks, tap_chunk, 0)
    last = 2 * chunks - 1
    keep_parts(begin_tile(0))
    first_conv = invert(parts[0], parts[1])
    keep_parts(begin_tile(1))
    finish_tile(0, first_conv)
    lax.fori_loop(1, last, forward_step, 0)
    last_conv = invert(parts[0], parts[1])
    tile_ends(last - 1, (0, 1))
    finish_tile(last, last_conv)
    send_ends(chunks - 2)
    tile_ends(last, (0, 1))
    send_ends(chunks - 1)
    pltpu.make_async_copy(esend.at[me], erecv.at[me], e_recv).start()

    amp[...] = resid[...] * jnp.sqrt(rate[...])
    z1[...] = jnp.exp(-rate[...])

    def lag_taps(ch):
        start = pl.multiple_of(ch * WIDE, WIDE)
        cols = pl.ds(start, WIDE)
        for m in range(MODES):
            zb[m, :, cols] = jnp.exp(-rate[m : m + 1, cols] * sub)
        highs, lows = [], []
        for group in range(2):
            lanes = pl.ds(start + group * LANES, LANES)
            power_of = [amp[m : m + 1, lanes] * zb[m, :, lanes] for m in range(MODES)]
            steps = [z8[m : m + 1, lanes] for m in range(MODES)]
            pieces = []
            for block in range(TILE // 8):
                total = power_of[0]
                for p in power_of[1:]:
                    total = total + p
                pieces.append(total)
                if block < TILE // 8 - 1:
                    power_of = [p * z for p, z in zip(power_of, steps)]
            wide = jnp.concatenate(pieces, axis=0)
            high = wide.astype(jnp.bfloat16)
            highs.append(high)
            lows.append((wide - high.astype(jnp.float32)).astype(jnp.bfloat16))
        return jnp.concatenate(highs, axis=1), jnp.concatenate(lows, axis=1)

    def products(ch, high, low):
        stacked = jnp.concatenate([high, high, low], axis=0)
        spectrum = jnp.dot(ahead[...], stacked, preferred_element_type=jnp.float32)
        return [product_of(transform(longin[half, ch]), spectrum) for half in range(2)]

    def keep_products(made):
        for half in range(2):
            parts[2 * half], parts[2 * half + 1] = made[half]

    def inside_chunk(ch):
        high, low = lag[0], lag[1]
        following = lag_taps(jnp.minimum(ch + 2, chunks - 1))
        done = [invert(parts[2 * half], parts[2 * half + 1]) for half in range(2)]
        made = products(jnp.minimum(ch + 1, chunks - 1), high, low)
        for half in range(2):
            inside[half, ch] = done[half]
        keep_products(made)
        lag[0], lag[1] = following

    opening = lag_taps(0)
    lag[0], lag[1] = lag_taps(1)
    keep_products(products(0, *opening))
    my_cols = pl.ds(pl.multiple_of((me // 2) * LANES, LANES), LANES)
    my_rate = rate[pl.ds(pl.multiple_of(8 * lax.rem(me, 2), 8), 8), my_cols]
    block_decay = jnp.exp(-2.0 * TILE * my_rate)
    slot = me // 4

    def scan_step(n, state):
        ssend[n] = state
        through = flag(jnp.logical_and(n > 0, docs[jnp.maximum(2 * n - 1, 0)] == docs[2 * n + 1]))
        return (block_decay * through) * state + erecv[n]

    def hand_back(step, carry):
        target = lax.rem(me + step, seq_count)
        pltpu.make_async_remote_copy(
            src_ref=ssend.at[target], dst_ref=srecv.at[me], send_sem=s_send, recv_sem=s_recv.at[slot],
            device_id=(target, part), device_id_type=MESH).start()
        return carry

    def middle_chunk(ch, carry):
        @pl.when(ch == 1 + (slot + 1) // 2)
        def _():
            wait_bytes(erecv, e_recv)
            lax.fori_loop(0, seq_count, scan_step, jnp.zeros((8, LANES), jnp.float32), unroll=8)
            lax.fori_loop(1, seq_count, hand_back, 0)
            pltpu.make_async_copy(ssend.at[me], srecv.at[me], s_recv.at[slot]).start()

        inside_chunk(ch)
        return carry

    lax.fori_loop(0, chunks, middle_chunk, 0)

    power[...] = jnp.zeros_like(power)

    def outward_chunk(ch, carry):
        start = pl.multiple_of(ch * WIDE, WIDE)
        tiles = pl.ds(pl.multiple_of(4 * ch, 4), 4)
        wait_bytes(srecv.at[tiles], s_recv.at[ch])
        for group in range(2):
            lanes = pl.ds(start + group * LANES, LANES)
            steps = [z8[m : m + 1, lanes] for m in range(MODES)]
            states = [kept0 * srecv[4 * ch + 2 * group + n] for n in range(2)]
            for half in range(2):
                if half == 1:
                    states = [
                        kept1 * (z128[8 * n : 8 * n + 8, lanes] * s + ends[0, 8 * n : 8 * n + 8, lanes])
                        for n, s in enumerate(states)
                    ]
                begun = [amp[8 * n : 8 * n + 8, lanes] * z1[8 * n : 8 * n + 8, lanes] * s for n, s in enumerate(states)]
                waves = [begun[m // 8][m % 8 : m % 8 + 1] * zb[m, :, lanes] for m in range(MODES)]
                for block in range(TILE // 8):
                    total = inside[half, ch, 8 * block : 8 * block + 8, group * LANES : (group + 1) * LANES]
                    for w in waves:
                        total = total + w
                    rows = pl.ds(half * TILE + 8 * block, 8)
                    total = total * q2[rows, lanes].astype(jnp.float32)
                    longout[rows, lanes] = total
                    power[rows, :] = power[rows, :] + total * total
                    if block < TILE // 8 - 1:
                        waves = [w * z for w, z in zip(waves, steps)]
        return carry

    lax.fori_loop(0, chunks, outward_chunk, 0)

    psend[...] = jnp.zeros_like(psend)
    for half in range(2):
        turned = power[half * TILE : (half + 1) * TILE, :].T
        psend[half : half + 1, :] = jnp.sum(turned, axis=0, keepdims=True)
    for step in range(1, mp_count):
        pltpu.make_async_remote_copy(
            src_ref=psend, dst_ref=precv.at[part], send_sem=p_send, recv_sem=p_recv,
            device_id=(me, lax.rem(part + step, mp_count)), device_id_type=MESH).start()
    precv[part] = psend[...]
    others = pl.ds(0, mp_count - 1)
    wait_bytes(precv.at[others], p_recv)
    total = precv[0]
    for n in range(1, mp_count):
        total = total + precv[n]
    scale = lax.rsqrt(total / (channels * mp_count) + norm_eps)
    for half in range(2):
        column = jnp.broadcast_to(scale[half : half + 1, :], (TILE, LANES)).T
        rows = pl.ds(half * TILE, TILE)
        for group in range(channels // LANES):
            lanes = slice(group * LANES, (group + 1) * LANES)
            outbuf[rows, lanes] = (longout[rows, lanes] * column).astype(jnp.bfloat16)

    wait_bytes(outgoing, halo_send)
    wait_bytes(esend.at[pl.ds(0, seq_count - 1)], e_send)
    wait_bytes(ssend.at[pl.ds(0, seq_count - 1)], s_send)
    wait_bytes(precv.at[others], p_send)


def on_device(mesh_sizes, values, k_first, q_first, k_second, q_second, mr_taps, li_rate, li_residue, tile_docs):
    seq_count, mp_count = mesh_sizes
    rows, channels = values.shape
    chunks = channels // WIDE
    ahead, pair, back = dft_tables()
    f32, bf16 = jnp.float32, jnp.bfloat16
    vmem = pltpu.VMEM
    hbm_spec = pl.BlockSpec(memory_space=pltpu.MemorySpace.HBM)
    big = vmem((rows, channels), bf16)
    modal = vmem((MODES, channels), f32)
    tiles = vmem((seq_count, 8, LANES), f32)
    dma = pltpu.SemaphoreType.DMA
    return pl.pallas_call(
        functools.partial(kernel, seq_count, mp_count),
        out_shape=vmem((rows, channels), bf16),
        in_specs=[pl.BlockSpec(memory_space=pltpu.SMEM)] + [hbm_spec] * 11,
        out_specs=pl.BlockSpec(memory_space=pltpu.VMEM),
        scratch_shapes=[
            big, big, big, big, big,
            vmem((TILE, channels), bf16),
            modal, modal,
            vmem(ahead.shape, bf16),
            vmem(pair.shape, bf16),
            vmem(back.shape, bf16),
            vmem((2, chunks, TILE, WIDE), bf16),
            vmem((2, chunks, TILE, WIDE), bf16),
            vmem((chunks, TILE, WIDE), bf16),
            vmem((2, chunks, TILE, WIDE), bf16),
            vmem((2, chunks, TILE, WIDE), f32),
            vmem((rows, channels), f32),
            modal, modal, modal, modal,
            vmem((MODES, 8, channels), f32),
            vmem((MODES, 8, channels), f32),
            vmem((chunks, 2 * TILE, WIDE), f32),
            vmem((4, 2 * TILE, WIDE), bf16),
            vmem((2, TILE, WIDE), bf16),
            vmem((2, MODES, channels), f32),
            tiles, tiles, tiles, tiles,
            vmem((rows, LANES), f32),
            vmem((8, LANES), f32),
            vmem((mp_count, 8, LANES), f32),
            dma((2, chunks)),
            dma((9,)),
            dma,
            dma((chunks,)),
            dma, dma, dma,
            dma((chunks,)),
            dma, dma,
        ],
        compiler_params=pltpu.CompilerParams(
            collective_id=0, has_side_effects=True, vmem_limit_bytes=56 * 1024 * 1024),
    )(tile_docs, values, k_first, q_first, k_second, q_second, mr_taps, li_rate, li_residue,
      jnp.asarray(ahead), jnp.asarray(pair), jnp.asarray(back))


def solution(mesh):
    sizes = (mesh.shape["seq"], mesh.shape["mp"])
    block = P("seq", "mp")
    param = P(None, "mp")
    return jax.shard_map(
        functools.partial(on_device, sizes),
        mesh=mesh,
        in_specs=(block, block, block, block, block, param, param, param, P()),
        out_specs=block,
        check_vma=False,
    )
```

```python
import functools
import jax
import jax.numpy as jnp
import numpy as np
from jax import lax
from jax.experimental import pallas as pl
from jax.experimental.pallas import tpu as pltpu
from jax.sharding import PartitionSpec as P

TILE = 128
MODES = 16
LANES = 128
WIDE = 256
norm_eps = 1e-06
MESH = pl.DeviceIdType.MESH


def split_bf16(table):
    high = table.astype(jnp.bfloat16)
    low = (table - high.astype(np.float64)).astype(jnp.bfloat16)
    return np.asarray(high), np.asarray(low)


def dft_tables():
    freq = 2.0 * np.pi * (4.0 * np.arange(TILE) + 1.0) / (4.0 * TILE)
    angle = freq[:, None] * np.arange(TILE)[None, :]
    real, imag = np.cos(angle), -np.sin(angle)

    def mixed(top, bottom):
        blocks = [part.reshape(TILE // 16, 1, 16, TILE) for part in (top, bottom)]
        return np.concatenate(blocks, axis=1).reshape(2 * TILE, TILE)

    current = mixed(real, imag)
    c_high, c_low = split_bf16(current)
    p_high, p_low = split_bf16(mixed(-imag, real))
    g_high, g_low = split_bf16(current.T / TILE)
    ahead = np.concatenate([c_high, c_low, c_high], axis=1)
    pair = np.concatenate([c_high, p_high, c_low, p_low], axis=1)
    back = np.concatenate([g_high, g_low], axis=0)
    return ahead, pair, back


def wait_bytes(ref, sem):
    pltpu.make_async_copy(ref, ref, sem).wait()


def parts_of(spectrum):
    blocks = spectrum.reshape(TILE // 16, 2, 16, WIDE)
    return blocks[:, 0], blocks[:, 1]


def woven(real, imag):
    return jnp.stack([real, imag], axis=1).reshape(2 * TILE, WIDE)


def kernel(
    seq_count, mp_count,
    docs, values_h, k1_h, q1_h, k2_h, q2_h, taps_h, rate_h, resid_h, ahead_h, pair_h, back_h,
    outbuf,
    values, k1, q1, k2, q2, taps, rate, resid, ahead, pair, back,
    tiles, longin, inside, longout, amp, z1, z8, z128, zb, zr,
    spectra, parts, lag, pairs, ends, esend, erecv, ssend, srecv, power, psend, precv,
    in_sem, par_sem, halo_send, halo_recv, e_send, e_recv, s_send, s_recv, p_send, p_recv,
):
    me = lax.axis_index("seq")
    part = lax.axis_index("mp")
    channels = values.shape[1]
    chunks = channels // WIDE

    def in_copy(source, target, row, ch):
        cols = pl.ds(ch * WIDE, WIDE)
        return pltpu.make_async_copy(source.at[:, cols], target.at[:, cols], in_sem.at[row, ch])

    whole = [(rate_h, rate), (resid_h, resid), (taps_h, taps), (ahead_h, ahead), (pair_h, pair), (back_h, back),
             (q1_h, q1), (k2_h, k2), (q2_h, q2)]
    whole_copies = [pltpu.make_async_copy(a, b, par_sem.at[n]) for n, (a, b) in enumerate(whole)]
    whole_copies[0].start()
    for ch in range(chunks):
        in_copy(values_h, values, 0, ch).start()
        in_copy(k1_h, k1, 1, ch).start()

    barrier = pltpu.get_barrier_semaphore()

    def greet(step, carry):
        pl.semaphore_signal(barrier, inc=1, device_id=(lax.rem(me + step, seq_count), part), device_id_type=MESH)
        return carry

    lax.fori_loop(1, seq_count, greet, 0)
    for step in range(1, mp_count):
        pl.semaphore_signal(barrier, inc=1, device_id=(me, lax.rem(part + step, mp_count)), device_id_type=MESH)

    for copy in whole_copies[1:]:
        copy.start()

    first = 2 * me
    doc_a = docs[first]
    doc_b = docs[first + 1]

    def flag(test):
        return jnp.where(test, 1.0, 0.0).astype(jnp.float32)

    kept0 = flag(jnp.logical_and(me > 0, docs[jnp.maximum(first - 1, 0)] == doc_a))
    kept1 = flag(doc_a == doc_b)

    whole_copies[0].wait()
    r_all = rate[...]
    z8[...] = jnp.exp(-8.0 * r_all)
    z128[...] = jnp.exp(-float(TILE) * r_all)
    sub = lax.broadcasted_iota(jnp.int32, (8, WIDE), 0).astype(jnp.float32)

    def fill_zr(ch, carry):
        cols = pl.ds(pl.multiple_of(ch * WIDE, WIDE), WIDE)
        for m in range(MODES):
            zr[m, :, cols] = jnp.exp(-rate[m : m + 1, cols] * (7.0 - sub))
        return carry

    lax.fori_loop(0, chunks, fill_zr, 0)

    for ch in range(chunks):
        in_copy(values_h, values, 0, ch).wait()
        in_copy(k1_h, k1, 1, ch).wait()
        cols = pl.ds(ch * WIDE, WIDE)
        rows = pl.ds(TILE, TILE)
        product = k1[rows, cols].astype(jnp.float32) * values[rows, cols].astype(jnp.float32)
        tiles[2, ch] = product.astype(jnp.bfloat16)

    pl.semaphore_wait(barrier, seq_count - 1 + mp_count - 1)
    after = lax.rem(me + 1, seq_count)

    for ch in range(chunks):
        pltpu.make_async_remote_copy(
            src_ref=tiles.at[2, ch], dst_ref=tiles.at[0, ch], send_sem=halo_send, recv_sem=halo_recv.at[ch],
            device_id=(after, part), device_id_type=MESH).start()

    for ch in range(chunks):
        cols = pl.ds(ch * WIDE, WIDE)
        rows = pl.ds(0, TILE)
        product = k1[rows, cols].astype(jnp.float32) * values[rows, cols].astype(jnp.float32)
        tiles[1, ch] = product.astype(jnp.bfloat16)

    for copy in whole_copies[1:]:
        copy.wait()
    for half, kept in enumerate((kept0, kept1)):
        for n in range(4):
            cols = slice(n * TILE, (n + 1) * TILE)
            block = pair[:, cols]
            pairs[half, :, cols] = (kept * block.astype(jnp.float32)).astype(jnp.bfloat16) if n % 2 else block

    def transform(tile):
        doubled = jnp.concatenate([tile, tile], axis=0)
        return jnp.dot(ahead[:, : 2 * TILE], doubled, preferred_element_type=jnp.float32)

    def product_of(spectrum, filter_spectrum):
        real, imag = parts_of(spectrum)
        s_real, s_imag = parts_of(filter_spectrum)
        product = woven(real * s_real - imag * s_imag, real * s_imag + imag * s_real)
        high = product.astype(jnp.bfloat16)
        low = (product - high.astype(jnp.float32)).astype(jnp.bfloat16)
        return high, low

    def invert(high, low):
        both = jnp.dot(back[...], high, preferred_element_type=jnp.float32)
        fine = jnp.dot(back[:TILE], low, preferred_element_type=jnp.float32)
        return both[:TILE] + (both[TILE:] + fine)

    def convolve(spectrum, filter_spectrum):
        return invert(*product_of(spectrum, filter_spectrum))

    def place_of(step):
        half = 1 - step // chunks
        ch = lax.rem(step, chunks)
        return half, ch, pl.multiple_of(ch * WIDE, WIDE)

    def begin_tile(step):
        half, ch, start = place_of(step)
        current, previous = tiles[half + 1, ch], tiles[half, ch]
        stacked = jnp.concatenate([current, previous, current, previous], axis=0)
        spectrum = jnp.dot(pairs[half], stacked, preferred_element_type=jnp.float32)
        return spectrum, spectra[ch]

    def keep_parts(begun):
        parts[0], parts[1] = product_of(*begun)

    def finish_tile(step, conv):
        half, ch, start = place_of(step)
        cols = pl.ds(start, WIDE)
        rows = pl.ds(pl.multiple_of(half * TILE, TILE), TILE)
        short = (q1[rows, cols].astype(jnp.float32) * conv).astype(jnp.bfloat16)
        longin[half, ch] = (k2[rows, cols].astype(jnp.float32) * short.astype(jnp.float32)).astype(jnp.bfloat16)

    def tile_ends(step, groups):
        half, ch, start = place_of(step)
        for group in groups:
            lanes = pl.ds(start + group * LANES, LANES)
            tile = longin[half, ch, :, group * LANES : (group + 1) * LANES].astype(jnp.float32)
            steps = [z8[m : m + 1, lanes] for m in range(MODES)]
            sums = [tile[0:8]] * MODES
            for block in range(1, TILE // 8):
                row = tile[8 * block : 8 * block + 8]
                sums = [s * z + row for s, z in zip(sums, steps)]
            for m, s in enumerate(sums):
                ends[half, m : m + 1, lanes] = jnp.sum(s * zr[m, :, lanes], axis=0, keepdims=True)

    def tap_chunk(ch, carry):
        spectra[ch] = transform(taps[:, pl.ds(pl.multiple_of(ch * WIDE, WIDE), WIDE)])
        return carry

    def send_ends(ch):
        for piece in range(4):
            owner = 4 * ch + piece
            lanes = pl.ds(pl.multiple_of(ch * WIDE, WIDE) + (piece // 2) * LANES, LANES)
            modes = pl.ds(8 * (piece % 2), 8)
            esend[owner] = ends[1, modes, lanes] + kept1 * z128[modes, lanes] * ends[0, modes, lanes]
        for piece in range(4):
            owner = 4 * ch + piece

            @pl.when(owner != me)
            def _():
                pltpu.make_async_remote_copy(
                    src_ref=esend.at[owner], dst_ref=erecv.at[me], send_sem=e_send, recv_sem=e_recv,
                    device_id=(owner, part), device_id_type=MESH).start()

    def side_by_side(step):
        tile_ends(step - 1, (0, 1))
        conv = invert(parts[0], parts[1])
        begun = begin_tile(step + 1)
        finish_tile(step, conv)
        keep_parts(begun)

    def forward_step(step, carry):
        @pl.when(step + 1 >= chunks)
        def _():
            ch = step + 1 - chunks
            wait_bytes(tiles.at[0, ch], halo_recv.at[ch])

        side_by_side(step)

        @pl.when(step - 1 >= chunks)
        def _():
            send_ends(step - 1 - chunks)

        return carry

    lax.fori_loop(0, chunks, tap_chunk, 0)
    last = 2 * chunks - 1
    keep_parts(begin_tile(0))
    first_conv = invert(parts[0], parts[1])
    keep_parts(begin_tile(1))
    finish_tile(0, first_conv)
    lax.fori_loop(1, last, forward_step, 0)
    last_conv = invert(parts[0], parts[1])
    tile_ends(last - 1, (0, 1))
    finish_tile(last, last_conv)
    send_ends(chunks - 2)
    tile_ends(last, (0, 1))
    send_ends(chunks - 1)
    pltpu.make_async_copy(esend.at[me], erecv.at[me], e_recv).start()

    amp[...] = resid[...] * jnp.sqrt(rate[...])
    z1[...] = jnp.exp(-rate[...])

    def lag_taps(ch):
        start = pl.multiple_of(ch * WIDE, WIDE)
        cols = pl.ds(start, WIDE)
        for m in range(MODES):
            zb[m, :, cols] = jnp.exp(-rate[m : m + 1, cols] * sub)
        highs, lows = [], []
        for group in range(2):
            lanes = pl.ds(start + group * LANES, LANES)
            power_of = [amp[m : m + 1, lanes] * zb[m, :, lanes] for m in range(MODES)]
            steps = [z8[m : m + 1, lanes] for m in range(MODES)]
            pieces = []
            for block in range(TILE // 8):
                total = power_of[0]
                for p in power_of[1:]:
                    total = total + p
                pieces.append(total)
                if block < TILE // 8 - 1:
                    power_of = [p * z for p, z in zip(power_of, steps)]
            wide = jnp.concatenate(pieces, axis=0)
            high = wide.astype(jnp.bfloat16)
            highs.append(high)
            lows.append((wide - high.astype(jnp.float32)).astype(jnp.bfloat16))
        return jnp.concatenate(highs, axis=1), jnp.concatenate(lows, axis=1)

    def products(ch, high, low):
        stacked = jnp.concatenate([high, high, low], axis=0)
        spectrum = jnp.dot(ahead[...], stacked, preferred_element_type=jnp.float32)
        return [product_of(transform(longin[half, ch]), spectrum) for half in range(2)]

    def keep_products(made):
        for half in range(2):
            parts[2 * half], parts[2 * half + 1] = made[half]

    def inside_chunk(ch):
        high, low = lag[0], lag[1]
        following = lag_taps(jnp.minimum(ch + 2, chunks - 1))
        made = products(jnp.minimum(ch + 1, chunks - 1), high, low)
        done = [invert(parts[2 * half], parts[2 * half + 1]) for half in range(2)]
        for half in range(2):
            inside[half, ch] = done[half]
        keep_products(made)
        lag[0], lag[1] = following

    opening = lag_taps(0)
    lag[0], lag[1] = lag_taps(1)
    keep_products(products(0, *opening))
    my_cols = pl.ds(pl.multiple_of((me // 2) * LANES, LANES), LANES)
    my_rate = rate[pl.ds(pl.multiple_of(8 * lax.rem(me, 2), 8), 8), my_cols]
    block_decay = jnp.exp(-2.0 * TILE * my_rate)
    slot = me // 4

    def scan_step(n, state):
        ssend[n] = state
        through = flag(jnp.logical_and(n > 0, docs[jnp.maximum(2 * n - 1, 0)] == docs[2 * n + 1]))
        return (block_decay * through) * state + erecv[n]

    def hand_back(step, carry):
        target = lax.rem(me + step, seq_count)
        pltpu.make_async_remote_copy(
            src_ref=ssend.at[target], dst_ref=srecv.at[me], send_sem=s_send, recv_sem=s_recv.at[slot],
            device_id=(target, part), device_id_type=MESH).start()
        return carry

    def middle_chunk(ch, carry):
        @pl.when(ch == 2 + slot // 2)
        def _():
            wait_bytes(erecv, e_recv)
            lax.fori_loop(0, seq_count, scan_step, jnp.zeros((8, LANES), jnp.float32), unroll=8)
            lax.fori_loop(1, seq_count, hand_back, 0)
            pltpu.make_async_copy(ssend.at[me], srecv.at[me], s_recv.at[slot]).start()

        inside_chunk(ch)
        return carry

    lax.fori_loop(0, chunks, middle_chunk, 0)

    power[...] = jnp.zeros_like(power)

    def outward_chunk(ch, carry):
        start = pl.multiple_of(ch * WIDE, WIDE)
        quad = pl.ds(pl.multiple_of(4 * ch, 4), 4)
        wait_bytes(srecv.at[quad], s_recv.at[ch])
        for group in range(2):
            lanes = pl.ds(start + group * LANES, LANES)
            steps = [z8[m : m + 1, lanes] for m in range(MODES)]
            states = [kept0 * srecv[4 * ch + 2 * group + n] for n in range(2)]
            for half in range(2):
                if half == 1:
                    states = [
                        kept1 * (z128[8 * n : 8 * n + 8, lanes] * s + ends[0, 8 * n : 8 * n + 8, lanes])
                        for n, s in enumerate(states)
                    ]
                begun = [amp[8 * n : 8 * n + 8, lanes] * z1[8 * n : 8 * n + 8, lanes] * s for n, s in enumerate(states)]
                waves = [begun[m // 8][m % 8 : m % 8 + 1] * zb[m, :, lanes] for m in range(MODES)]
                for block in range(TILE // 8):
                    total = inside[half, ch, 8 * block : 8 * block + 8, group * LANES : (group + 1) * LANES]
                    for w in waves:
                        total = total + w
                    rows = pl.ds(half * TILE + 8 * block, 8)
                    total = total * q2[rows, lanes].astype(jnp.float32)
                    longout[rows, lanes] = total
                    power[rows, :] = power[rows, :] + total * total
                    if block < TILE // 8 - 1:
                        waves = [w * z for w, z in zip(waves, steps)]
        return carry

    lax.fori_loop(0, chunks, outward_chunk, 0)

    psend[...] = jnp.zeros_like(psend)
    for half in range(2):
        turned = power[half * TILE : (half + 1) * TILE, :].T
        psend[half : half + 1, :] = jnp.sum(turned, axis=0, keepdims=True)
    for step in range(1, mp_count):
        pltpu.make_async_remote_copy(
            src_ref=psend, dst_ref=precv.at[part], send_sem=p_send, recv_sem=p_recv,
            device_id=(me, lax.rem(part + step, mp_count)), device_id_type=MESH).start()
    precv[part] = psend[...]
    others = pl.ds(0, mp_count - 1)
    wait_bytes(precv.at[others], p_recv)
    total = precv[0]
    for n in range(1, mp_count):
        total = total + precv[n]
    scale = lax.rsqrt(total / (channels * mp_count) + norm_eps)
    for half in range(2):
        column = jnp.broadcast_to(scale[half : half + 1, :], (TILE, LANES)).T
        rows = pl.ds(half * TILE, TILE)
        for group in range(channels // LANES):
            lanes = slice(group * LANES, (group + 1) * LANES)
            outbuf[rows, lanes] = (longout[rows, lanes] * column).astype(jnp.bfloat16)

    wait_bytes(tiles.at[2], halo_send)
    wait_bytes(esend.at[pl.ds(0, seq_count - 1)], e_send)
    wait_bytes(ssend.at[pl.ds(0, seq_count - 1)], s_send)
    wait_bytes(precv.at[others], p_send)


def on_device(mesh_sizes, values, k_first, q_first, k_second, q_second, mr_taps, li_rate, li_residue, tile_docs):
    seq_count, mp_count = mesh_sizes
    rows, channels = values.shape
    chunks = channels // WIDE
    ahead, pair, back = dft_tables()
    f32, bf16 = jnp.float32, jnp.bfloat16
    vmem = pltpu.VMEM
    hbm_spec = pl.BlockSpec(memory_space=pltpu.MemorySpace.HBM)
    big = vmem((rows, channels), bf16)
    modal = vmem((MODES, channels), f32)
    tiles = vmem((seq_count, 8, LANES), f32)
    dma = pltpu.SemaphoreType.DMA
    return pl.pallas_call(
        functools.partial(kernel, seq_count, mp_count),
        out_shape=vmem((rows, channels), bf16),
        in_specs=[pl.BlockSpec(memory_space=pltpu.SMEM)] + [hbm_spec] * 11,
        out_specs=pl.BlockSpec(memory_space=pltpu.VMEM),
        scratch_shapes=[
            big, big, big, big, big,
            vmem((TILE, channels), bf16),
            modal, modal,
            vmem(ahead.shape, bf16),
            vmem(pair.shape, bf16),
            vmem(back.shape, bf16),
            vmem((3, chunks, TILE, WIDE), bf16),
            vmem((2, chunks, TILE, WIDE), bf16),
            vmem((2, chunks, TILE, WIDE), f32),
            vmem((rows, channels), f32),
            modal, modal, modal, modal,
            vmem((MODES, 8, channels), f32),
            vmem((MODES, 8, channels), f32),
            vmem((chunks, 2 * TILE, WIDE), f32),
            vmem((4, 2 * TILE, WIDE), bf16),
            vmem((2, TILE, WIDE), bf16),
            vmem((2,) + pair.shape, bf16),
            vmem((2, MODES, channels), f32),
            tiles, tiles, tiles, tiles,
            vmem((rows, LANES), f32),
            vmem((8, LANES), f32),
            vmem((mp_count, 8, LANES), f32),
            dma((2, chunks)),
            dma((9,)),
            dma,
            dma((chunks,)),
            dma, dma, dma,
            dma((chunks,)),
            dma, dma,
        ],
        compiler_params=pltpu.CompilerParams(
            collective_id=0, has_side_effects=True, vmem_limit_bytes=56 * 1024 * 1024),
    )(tile_docs, values, k_first, q_first, k_second, q_second, mr_taps, li_rate, li_residue,
      jnp.asarray(ahead), jnp.asarray(pair), jnp.asarray(back))


def solution(mesh):
    sizes = (mesh.shape["seq"], mesh.shape["mp"])
    block = P("seq", "mp")
    param = P(None, "mp")
    return jax.shard_map(
        functools.partial(on_device, sizes),
        mesh=mesh,
        in_specs=(block, block, block, block, block, param, param, param, P()),
        out_specs=block,
        check_vma=False,
    )
```

```python
import functools
import jax
import jax.numpy as jnp
import numpy as np
from jax import lax
from jax.experimental import pallas as pl
from jax.experimental.pallas import tpu as pltpu
from jax.sharding import PartitionSpec as P

TILE = 128
MODES = 16
LANES = 128
WIDE = 256
norm_eps = 1e-06
MESH = pl.DeviceIdType.MESH


def split_bf16(table):
    high = table.astype(jnp.bfloat16)
    low = (table - high.astype(np.float64)).astype(jnp.bfloat16)
    return np.asarray(high), np.asarray(low)


def dft_tables():
    freq = 2.0 * np.pi * (4.0 * np.arange(TILE) + 1.0) / (4.0 * TILE)
    angle = freq[:, None] * np.arange(TILE)[None, :]
    real, imag = np.cos(angle), -np.sin(angle)

    def mixed(top, bottom):
        blocks = [part.reshape(TILE // 16, 1, 16, TILE) for part in (top, bottom)]
        return np.concatenate(blocks, axis=1).reshape(2 * TILE, TILE)

    current = mixed(real, imag)
    c_high, c_low = split_bf16(current)
    p_high, p_low = split_bf16(mixed(-imag, real))
    g_high, g_low = split_bf16(current.T / TILE)
    ahead = np.concatenate([c_high, c_low, c_high], axis=1)
    pair = np.concatenate([c_high, p_high, c_low, p_low], axis=1)
    back = np.concatenate([g_high, g_low], axis=0)
    return ahead, pair, back


def wait_bytes(ref, sem):
    pltpu.make_async_copy(ref, ref, sem).wait()


def parts_of(spectrum):
    blocks = spectrum.reshape(TILE // 16, 2, 16, WIDE)
    return blocks[:, 0], blocks[:, 1]


def woven(real, imag):
    return jnp.stack([real, imag], axis=1).reshape(2 * TILE, WIDE)


def kernel(
    seq_count, mp_count,
    docs, values_h, k1_h, q1_h, k2_h, q2_h, taps_h, rate_h, resid_h, ahead_h, pair_h, back_h,
    outbuf,
    values, k1, q1, k2, q2, taps, rate, resid, ahead, pair, back,
    tiles, longin, inside, longout, amp, z1, z8, z128, zb, zr,
    spectra, parts, lag, pairs, ends, esend, erecv, ssend, srecv, power, psend, precv,
    in_sem, par_sem, halo_send, halo_recv, e_send, e_recv, s_send, s_recv, p_send, p_recv,
):
    me = lax.axis_index("seq")
    part = lax.axis_index("mp")
    channels = values.shape[1]
    chunks = channels // WIDE

    def in_copies(half, ch):
        place = (pl.ds(half * TILE, TILE), pl.ds(ch * WIDE, WIDE))
        return [
            pltpu.make_async_copy(source.at[place], target.at[place], in_sem.at[2 * half + n, ch])
            for n, (source, target) in enumerate(((values_h, values), (k1_h, k1)))
        ]

    whole = [(rate_h, rate), (resid_h, resid), (taps_h, taps), (ahead_h, ahead), (pair_h, pair), (back_h, back),
             (q1_h, q1), (k2_h, k2), (q2_h, q2)]
    whole_copies = [pltpu.make_async_copy(a, b, par_sem.at[n]) for n, (a, b) in enumerate(whole)]
    for ch in range(chunks):
        for copy in in_copies(1, ch):
            copy.start()

    barrier = pltpu.get_barrier_semaphore()

    def greet(step, carry):
        pl.semaphore_signal(barrier, inc=1, device_id=(lax.rem(me + step, seq_count), part), device_id_type=MESH)
        return carry

    lax.fori_loop(1, seq_count, greet, 0)
    for step in range(1, mp_count):
        pl.semaphore_signal(barrier, inc=1, device_id=(me, lax.rem(part + step, mp_count)), device_id_type=MESH)

    whole_copies[0].start()
    for ch in range(chunks):
        for copy in in_copies(0, ch):
            copy.start()
    for copy in whole_copies[1:]:
        copy.start()

    first = 2 * me
    doc_a = docs[first]
    doc_b = docs[first + 1]

    def flag(test):
        return jnp.where(test, 1.0, 0.0).astype(jnp.float32)

    kept0 = flag(jnp.logical_and(me > 0, docs[jnp.maximum(first - 1, 0)] == doc_a))
    kept1 = flag(doc_a == doc_b)

    def gate(half, ch):
        for copy in in_copies(half, ch):
            copy.wait()
        cols = pl.ds(ch * WIDE, WIDE)
        rows = pl.ds(half * TILE, TILE)
        product = k1[rows, cols].astype(jnp.float32) * values[rows, cols].astype(jnp.float32)
        tiles[half + 1, ch] = product.astype(jnp.bfloat16)

    gate(1, 0)
    pl.semaphore_wait(barrier, seq_count - 1 + mp_count - 1)
    after = lax.rem(me + 1, seq_count)

    for ch in range(chunks):
        if ch + 1 < chunks:
            gate(1, ch + 1)
        pltpu.make_async_remote_copy(
            src_ref=tiles.at[2, ch], dst_ref=tiles.at[0, ch], send_sem=halo_send, recv_sem=halo_recv.at[ch],
            device_id=(after, part), device_id_type=MESH).start()

    for ch in range(chunks):
        gate(0, ch)

    whole_copies[0].wait()
    r_all = rate[...]
    z8[...] = jnp.exp(-8.0 * r_all)
    z128[...] = jnp.exp(-float(TILE) * r_all)
    sub = lax.broadcasted_iota(jnp.int32, (8, WIDE), 0).astype(jnp.float32)

    def fill_zr(ch, carry):
        cols = pl.ds(pl.multiple_of(ch * WIDE, WIDE), WIDE)
        for m in range(MODES):
            zr[m, :, cols] = jnp.exp(-rate[m : m + 1, cols] * (7.0 - sub))
        return carry

    lax.fori_loop(0, chunks, fill_zr, 0)

    for copy in whole_copies[1:]:
        copy.wait()
    for half, kept in enumerate((kept0, kept1)):
        for n in range(4):
            cols = slice(n * TILE, (n + 1) * TILE)
            block = pair[:, cols]
            pairs[half, :, cols] = (kept * block.astype(jnp.float32)).astype(jnp.bfloat16) if n % 2 else block

    def transform(tile):
        doubled = jnp.concatenate([tile, tile], axis=0)
        return jnp.dot(ahead[:, : 2 * TILE], doubled, preferred_element_type=jnp.float32)

    def product_of(spectrum, filter_spectrum):
        real, imag = parts_of(spectrum)
        s_real, s_imag = parts_of(filter_spectrum)
        product = woven(real * s_real - imag * s_imag, real * s_imag + imag * s_real)
        high = product.astype(jnp.bfloat16)
        low = (product - high.astype(jnp.float32)).astype(jnp.bfloat16)
        return high, low

    def invert(high, low):
        both = jnp.dot(back[...], high, preferred_element_type=jnp.float32)
        fine = jnp.dot(back[:TILE], low, preferred_element_type=jnp.float32)
        return both[:TILE] + (both[TILE:] + fine)

    def convolve(spectrum, filter_spectrum):
        return invert(*product_of(spectrum, filter_spectrum))

    def place_of(step):
        half = 1 - step // chunks
        ch = lax.rem(step, chunks)
        return half, ch, pl.multiple_of(ch * WIDE, WIDE)

    def begin_tile(step):
        half, ch, start = place_of(step)
        current, previous = tiles[half + 1, ch], tiles[half, ch]
        stacked = jnp.concatenate([current, previous, current, previous], axis=0)
        spectrum = jnp.dot(pairs[half], stacked, preferred_element_type=jnp.float32)
        return spectrum, spectra[ch]

    def keep_parts(begun):
        parts[0], parts[1] = product_of(*begun)

    def finish_tile(step, conv):
        half, ch, start = place_of(step)
        cols = pl.ds(start, WIDE)
        rows = pl.ds(pl.multiple_of(half * TILE, TILE), TILE)
        short = (q1[rows, cols].astype(jnp.float32) * conv).astype(jnp.bfloat16)
        longin[half, ch] = (k2[rows, cols].astype(jnp.float32) * short.astype(jnp.float32)).astype(jnp.bfloat16)

    def tile_ends(step, groups):
        half, ch, start = place_of(step)
        for group in groups:
            lanes = pl.ds(start + group * LANES, LANES)
            tile = longin[half, ch, :, group * LANES : (group + 1) * LANES].astype(jnp.float32)
            steps = [z8[m : m + 1, lanes] for m in range(MODES)]
            sums = [tile[0:8]] * MODES
            for block in range(1, TILE // 8):
                row = tile[8 * block : 8 * block + 8]
                sums = [s * z + row for s, z in zip(sums, steps)]
            for m, s in enumerate(sums):
                ends[half, m : m + 1, lanes] = jnp.sum(s * zr[m, :, lanes], axis=0, keepdims=True)

    def tap_chunk(ch, carry):
        spectra[ch] = transform(taps[:, pl.ds(pl.multiple_of(ch * WIDE, WIDE), WIDE)])
        return carry

    def send_ends(ch):
        for piece in range(4):
            owner = 4 * ch + piece
            lanes = pl.ds(pl.multiple_of(ch * WIDE, WIDE) + (piece // 2) * LANES, LANES)
            modes = pl.ds(8 * (piece % 2), 8)
            esend[owner] = ends[1, modes, lanes] + kept1 * z128[modes, lanes] * ends[0, modes, lanes]
        for piece in range(4):
            owner = 4 * ch + piece

            @pl.when(owner != me)
            def _():
                pltpu.make_async_remote_copy(
                    src_ref=esend.at[owner], dst_ref=erecv.at[me], send_sem=e_send, recv_sem=e_recv,
                    device_id=(owner, part), device_id_type=MESH).start()

    def side_by_side(step):
        tile_ends(step - 1, (0, 1))
        conv = invert(parts[0], parts[1])
        begun = begin_tile(step + 1)
        finish_tile(step, conv)
        keep_parts(begun)

    def forward_step(step, carry):
        @pl.when(step + 1 >= chunks)
        def _():
            ch = step + 1 - chunks
            wait_bytes(tiles.at[0, ch], halo_recv.at[ch])

        side_by_side(step)

        @pl.when(step - 1 >= chunks)
        def _():
            send_ends(step - 1 - chunks)

        return carry

    lax.fori_loop(0, chunks, tap_chunk, 0)
    last = 2 * chunks - 1
    keep_parts(begin_tile(0))
    first_conv = invert(parts[0], parts[1])
    keep_parts(begin_tile(1))
    finish_tile(0, first_conv)
    lax.fori_loop(1, last, forward_step, 0)
    last_conv = invert(parts[0], parts[1])
    tile_ends(last - 1, (0, 1))
    finish_tile(last, last_conv)
    send_ends(chunks - 2)
    tile_ends(last, (0, 1))
    send_ends(chunks - 1)
    pltpu.make_async_copy(esend.at[me], erecv.at[me], e_recv).start()

    amp[...] = resid[...] * jnp.sqrt(rate[...])
    z1[...] = jnp.exp(-rate[...])

    def lag_taps(ch):
        start = pl.multiple_of(ch * WIDE, WIDE)
        cols = pl.ds(start, WIDE)
        for m in range(MODES):
            zb[m, :, cols] = jnp.exp(-rate[m : m + 1, cols] * sub)
        highs, lows = [], []
        for group in range(2):
            lanes = pl.ds(start + group * LANES, LANES)
            power_of = [amp[m : m + 1, lanes] * zb[m, :, lanes] for m in range(MODES)]
            steps = [z8[m : m + 1, lanes] for m in range(MODES)]
            pieces = []
            for block in range(TILE // 8):
                total = power_of[0]
                for p in power_of[1:]:
                    total = total + p
                pieces.append(total)
                if block < TILE // 8 - 1:
                    power_of = [p * z for p, z in zip(power_of, steps)]
            wide = jnp.concatenate(pieces, axis=0)
            high = wide.astype(jnp.bfloat16)
            highs.append(high)
            lows.append((wide - high.astype(jnp.float32)).astype(jnp.bfloat16))
        return jnp.concatenate(highs, axis=1), jnp.concatenate(lows, axis=1)

    def products(ch, high, low):
        stacked = jnp.concatenate([high, high, low], axis=0)
        spectrum = jnp.dot(ahead[...], stacked, preferred_element_type=jnp.float32)
        return [product_of(transform(longin[half, ch]), spectrum) for half in range(2)]

    def keep_products(made):
        for half in range(2):
            parts[2 * half], parts[2 * half + 1] = made[half]

    def inside_chunk(ch):
        high, low = lag[0], lag[1]
        following = lag_taps(jnp.minimum(ch + 2, chunks - 1))
        made = products(jnp.minimum(ch + 1, chunks - 1), high, low)
        done = [invert(parts[2 * half], parts[2 * half + 1]) for half in range(2)]
        for half in range(2):
            inside[half, ch] = done[half]
        keep_products(made)
        lag[0], lag[1] = following

    opening = lag_taps(0)
    lag[0], lag[1] = lag_taps(1)
    keep_products(products(0, *opening))
    my_cols = pl.ds(pl.multiple_of((me // 2) * LANES, LANES), LANES)
    my_rate = rate[pl.ds(pl.multiple_of(8 * lax.rem(me, 2), 8), 8), my_cols]
    block_decay = jnp.exp(-2.0 * TILE * my_rate)
    slot = me // 4

    def scan_step(n, state):
        ssend[n] = state
        through = flag(jnp.logical_and(n > 0, docs[jnp.maximum(2 * n - 1, 0)] == docs[2 * n + 1]))
        return (block_decay * through) * state + erecv[n]

    def hand_back(step, carry):
        target = lax.rem(me + step, seq_count)
        pltpu.make_async_remote_copy(
            src_ref=ssend.at[target], dst_ref=srecv.at[me], send_sem=s_send, recv_sem=s_recv.at[slot],
            device_id=(target, part), device_id_type=MESH).start()
        return carry

    def middle_chunk(ch, carry):
        @pl.when(ch == 2 + slot // 2)
        def _():
            wait_bytes(erecv, e_recv)
            lax.fori_loop(0, seq_count, scan_step, jnp.zeros((8, LANES), jnp.float32), unroll=8)
            lax.fori_loop(1, seq_count, hand_back, 0)
            pltpu.make_async_copy(ssend.at[me], srecv.at[me], s_recv.at[slot]).start()

        inside_chunk(ch)
        return carry

    lax.fori_loop(0, chunks, middle_chunk, 0)

    power[...] = jnp.zeros_like(power)

    def outward_chunk(ch, carry):
        start = pl.multiple_of(ch * WIDE, WIDE)
        quad = pl.ds(pl.multiple_of(4 * ch, 4), 4)
        wait_bytes(srecv.at[quad], s_recv.at[ch])
        for group in range(2):
            lanes = pl.ds(start + group * LANES, LANES)
            steps = [z8[m : m + 1, lanes] for m in range(MODES)]
            states = [kept0 * srecv[4 * ch + 2 * group + n] for n in range(2)]
            for half in range(2):
                if half == 1:
                    states = [
                        kept1 * (z128[8 * n : 8 * n + 8, lanes] * s + ends[0, 8 * n : 8 * n + 8, lanes])
                        for n, s in enumerate(states)
                    ]
                begun = [amp[8 * n : 8 * n + 8, lanes] * z1[8 * n : 8 * n + 8, lanes] * s for n, s in enumerate(states)]
                waves = [begun[m // 8][m % 8 : m % 8 + 1] * zb[m, :, lanes] for m in range(MODES)]
                for block in range(TILE // 8):
                    total = inside[half, ch, 8 * block : 8 * block + 8, group * LANES : (group + 1) * LANES]
                    for w in waves:
                        total = total + w
                    rows = pl.ds(half * TILE + 8 * block, 8)
                    total = total * q2[rows, lanes].astype(jnp.float32)
                    longout[rows, lanes] = total
                    power[rows, :] = power[rows, :] + total * total
                    if block < TILE // 8 - 1:
                        waves = [w * z for w, z in zip(waves, steps)]
        return carry

    lax.fori_loop(0, chunks, outward_chunk, 0)

    psend[...] = jnp.zeros_like(psend)
    for half in range(2):
        turned = power[half * TILE : (half + 1) * TILE, :].T
        psend[half : half + 1, :] = jnp.sum(turned, axis=0, keepdims=True)
    for step in range(1, mp_count):
        pltpu.make_async_remote_copy(
            src_ref=psend, dst_ref=precv.at[part], send_sem=p_send, recv_sem=p_recv,
            device_id=(me, lax.rem(part + step, mp_count)), device_id_type=MESH).start()
    precv[part] = psend[...]
    others = pl.ds(0, mp_count - 1)
    wait_bytes(precv.at[others], p_recv)
    total = precv[0]
    for n in range(1, mp_count):
        total = total + precv[n]
    scale = lax.rsqrt(total / (channels * mp_count) + norm_eps)
    for half in range(2):
        column = jnp.broadcast_to(scale[half : half + 1, :], (TILE, LANES)).T
        rows = pl.ds(half * TILE, TILE)
        for group in range(channels // LANES):
            lanes = slice(group * LANES, (group + 1) * LANES)
            outbuf[rows, lanes] = (longout[rows, lanes] * column).astype(jnp.bfloat16)

    wait_bytes(tiles.at[2], halo_send)
    wait_bytes(esend.at[pl.ds(0, seq_count - 1)], e_send)
    wait_bytes(ssend.at[pl.ds(0, seq_count - 1)], s_send)
    wait_bytes(precv.at[others], p_send)


def on_device(mesh_sizes, values, k_first, q_first, k_second, q_second, mr_taps, li_rate, li_residue, tile_docs):
    seq_count, mp_count = mesh_sizes
    rows, channels = values.shape
    chunks = channels // WIDE
    ahead, pair, back = dft_tables()
    f32, bf16 = jnp.float32, jnp.bfloat16
    vmem = pltpu.VMEM
    hbm_spec = pl.BlockSpec(memory_space=pltpu.MemorySpace.HBM)
    big = vmem((rows, channels), bf16)
    modal = vmem((MODES, channels), f32)
    tiles = vmem((seq_count, 8, LANES), f32)
    dma = pltpu.SemaphoreType.DMA
    return pl.pallas_call(
        functools.partial(kernel, seq_count, mp_count),
        out_shape=vmem((rows, channels), bf16),
        in_specs=[pl.BlockSpec(memory_space=pltpu.SMEM)] + [hbm_spec] * 11,
        out_specs=pl.BlockSpec(memory_space=pltpu.VMEM),
        scratch_shapes=[
            big, big, big, big, big,
            vmem((TILE, channels), bf16),
            modal, modal,
            vmem(ahead.shape, bf16),
            vmem(pair.shape, bf16),
            vmem(back.shape, bf16),
            vmem((3, chunks, TILE, WIDE), bf16),
            vmem((2, chunks, TILE, WIDE), bf16),
            vmem((2, chunks, TILE, WIDE), f32),
            vmem((rows, channels), f32),
            modal, modal, modal, modal,
            vmem((MODES, 8, channels), f32),
            vmem((MODES, 8, channels), f32),
            vmem((chunks, 2 * TILE, WIDE), f32),
            vmem((4, 2 * TILE, WIDE), bf16),
            vmem((2, TILE, WIDE), bf16),
            vmem((2,) + pair.shape, bf16),
            vmem((2, MODES, channels), f32),
            tiles, tiles, tiles, tiles,
            vmem((rows, LANES), f32),
            vmem((8, LANES), f32),
            vmem((mp_count, 8, LANES), f32),
            dma((4, chunks)),
            dma((9,)),
            dma,
            dma((chunks,)),
            dma, dma, dma,
            dma((chunks,)),
            dma, dma,
        ],
        compiler_params=pltpu.CompilerParams(
            collective_id=0, has_side_effects=True, vmem_limit_bytes=56 * 1024 * 1024),
    )(tile_docs, values, k_first, q_first, k_second, q_second, mr_taps, li_rate, li_residue,
      jnp.asarray(ahead), jnp.asarray(pair), jnp.asarray(back))


def solution(mesh):
    sizes = (mesh.shape["seq"], mesh.shape["mp"])
    block = P("seq", "mp")
    param = P(None, "mp")
    return jax.shard_map(
        functools.partial(on_device, sizes),
        mesh=mesh,
        in_specs=(block, block, block, block, block, param, param, param, P()),
        out_specs=block,
        check_vma=False,
    )
```

```python
import functools
import jax
import jax.numpy as jnp
import numpy as np
from jax import lax
from jax.experimental import pallas as pl
from jax.experimental.pallas import tpu as pltpu
from jax.sharding import PartitionSpec as P

TILE = 128
MODES = 16
LANES = 128
WIDE = 256
norm_eps = 1e-06
MESH = pl.DeviceIdType.MESH


def split_bf16(table):
    high = table.astype(jnp.bfloat16)
    low = (table - high.astype(np.float64)).astype(jnp.bfloat16)
    return np.asarray(high), np.asarray(low)


def dft_tables():
    freq = 2.0 * np.pi * (4.0 * np.arange(TILE) + 1.0) / (4.0 * TILE)
    angle = freq[:, None] * np.arange(TILE)[None, :]
    real, imag = np.cos(angle), -np.sin(angle)

    def mixed(top, bottom):
        blocks = [part.reshape(TILE // 16, 1, 16, TILE) for part in (top, bottom)]
        return np.concatenate(blocks, axis=1).reshape(2 * TILE, TILE)

    current = mixed(real, imag)
    c_high, c_low = split_bf16(current)
    p_high, p_low = split_bf16(mixed(-imag, real))
    g_high, g_low = split_bf16(current.T / TILE)
    ahead = np.concatenate([c_high, c_low, c_high], axis=1)
    pair = np.concatenate([c_high, p_high, c_low, p_low], axis=1)
    back = np.concatenate([g_high, g_low], axis=0)
    return ahead, pair, back


def wait_bytes(ref, sem):
    pltpu.make_async_copy(ref, ref, sem).wait()


def parts_of(spectrum):
    blocks = spectrum.reshape(TILE // 16, 2, 16, WIDE)
    return blocks[:, 0], blocks[:, 1]


def woven(real, imag):
    return jnp.stack([real, imag], axis=1).reshape(2 * TILE, WIDE)


def kernel(
    seq_count, mp_count,
    docs, values_h, k1_h, q1_h, k2_h, q2_h, taps_h, rate_h, resid_h, ahead_h, pair_h, back_h,
    outbuf,
    values, k1, q1, k2, q2, taps, rate, resid, ahead, pair, back,
    tiles, longin, inside, longout, amp, z1, z8, z128, zb, zr,
    spectra, parts, lag, pairs, ends, esend, erecv, ssend, srecv, power, psend, precv,
    in_sem, par_sem, halo_send, halo_recv, e_send, e_recv, s_send, s_recv, p_send, p_recv,
):
    me = lax.axis_index("seq")
    part = lax.axis_index("mp")
    channels = values.shape[1]
    chunks = channels // WIDE

    def in_copies(half, ch):
        place = (pl.ds(half * TILE, TILE), pl.ds(ch * WIDE, WIDE))
        return [
            pltpu.make_async_copy(source.at[place], target.at[place], in_sem.at[2 * half + n, ch])
            for n, (source, target) in enumerate(((values_h, values), (k1_h, k1)))
        ]

    whole = [(rate_h, rate), (resid_h, resid), (taps_h, taps), (ahead_h, ahead), (pair_h, pair), (back_h, back),
             (q1_h, q1), (k2_h, k2), (q2_h, q2)]
    whole_copies = [pltpu.make_async_copy(a, b, par_sem.at[n]) for n, (a, b) in enumerate(whole)]
    for ch in range(chunks):
        for copy in in_copies(1, ch):
            copy.start()

    barrier = pltpu.get_barrier_semaphore()

    def greet(step, carry):
        pl.semaphore_signal(barrier, inc=1, device_id=(lax.rem(me + step, seq_count), part), device_id_type=MESH)
        return carry

    lax.fori_loop(1, seq_count, greet, 0)
    for step in range(1, mp_count):
        pl.semaphore_signal(barrier, inc=1, device_id=(me, lax.rem(part + step, mp_count)), device_id_type=MESH)

    whole_copies[0].start()
    for ch in range(chunks):
        for copy in in_copies(0, ch):
            copy.start()
    for copy in whole_copies[1:]:
        copy.start()

    first = 2 * me
    doc_a = docs[first]
    doc_b = docs[first + 1]

    def flag(test):
        return jnp.where(test, 1.0, 0.0).astype(jnp.float32)

    kept0 = flag(jnp.logical_and(me > 0, docs[jnp.maximum(first - 1, 0)] == doc_a))
    kept1 = flag(doc_a == doc_b)

    def gate(half, ch):
        for copy in in_copies(half, ch):
            copy.wait()
        cols = pl.ds(ch * WIDE, WIDE)
        rows = pl.ds(half * TILE, TILE)
        product = k1[rows, cols].astype(jnp.float32) * values[rows, cols].astype(jnp.float32)
        tiles[half + 1, ch] = product.astype(jnp.bfloat16)

    gate(1, 0)
    pl.semaphore_wait(barrier, seq_count - 1 + mp_count - 1)
    after = lax.rem(me + 1, seq_count)

    for ch in range(chunks):
        if ch + 1 < chunks:
            gate(1, ch + 1)
        pltpu.make_async_remote_copy(
            src_ref=tiles.at[2, ch], dst_ref=tiles.at[0, ch], send_sem=halo_send, recv_sem=halo_recv.at[ch],
            device_id=(after, part), device_id_type=MESH).start()

    for ch in range(chunks):
        gate(0, ch)

    whole_copies[0].wait()
    r_all = rate[...]
    z8[...] = jnp.exp(-8.0 * r_all)
    z128[...] = jnp.exp(-float(TILE) * r_all)
    sub = lax.broadcasted_iota(jnp.int32, (8, WIDE), 0).astype(jnp.float32)

    def fill_zr(ch, carry):
        cols = pl.ds(pl.multiple_of(ch * WIDE, WIDE), WIDE)
        for m in range(MODES):
            zr[m, :, cols] = jnp.exp(-rate[m : m + 1, cols] * (7.0 - sub))
        return carry

    lax.fori_loop(0, chunks, fill_zr, 0)

    for copy in whole_copies[1:]:
        copy.wait()
    for half, kept in enumerate((kept0, kept1)):
        for n in range(4):
            cols = slice(n * TILE, (n + 1) * TILE)
            block = pair[:, cols]
            pairs[half, :, cols] = (kept * block.astype(jnp.float32)).astype(jnp.bfloat16) if n % 2 else block

    def transform(tile):
        doubled = jnp.concatenate([tile, tile], axis=0)
        return jnp.dot(ahead[:, : 2 * TILE], doubled, preferred_element_type=jnp.float32)

    def product_of(spectrum, filter_spectrum):
        real, imag = parts_of(spectrum)
        s_real, s_imag = parts_of(filter_spectrum)
        product = woven(real * s_real - imag * s_imag, real * s_imag + imag * s_real)
        high = product.astype(jnp.bfloat16)
        low = (product - high.astype(jnp.float32)).astype(jnp.bfloat16)
        return high, low

    def invert(high, low):
        both = jnp.dot(back[...], high, preferred_element_type=jnp.float32)
        fine = jnp.dot(back[:TILE], low, preferred_element_type=jnp.float32)
        return both[:TILE] + (both[TILE:] + fine)

    def convolve(spectrum, filter_spectrum):
        return invert(*product_of(spectrum, filter_spectrum))

    def place_of(step):
        half = 1 - step // chunks
        ch = lax.rem(step, chunks)
        return half, ch, pl.multiple_of(ch * WIDE, WIDE)

    def begin_tile(step):
        half, ch, start = place_of(step)
        current, previous = tiles[half + 1, ch], tiles[half, ch]
        stacked = jnp.concatenate([current, previous, current, previous], axis=0)
        spectrum = jnp.dot(pairs[half], stacked, preferred_element_type=jnp.float32)
        return spectrum, spectra[ch]

    def keep_parts(begun):
        parts[0], parts[1] = product_of(*begun)

    def finish_tile(step, conv):
        half, ch, start = place_of(step)
        cols = pl.ds(start, WIDE)
        rows = pl.ds(pl.multiple_of(half * TILE, TILE), TILE)
        short = (q1[rows, cols].astype(jnp.float32) * conv).astype(jnp.bfloat16)
        longin[half, ch] = (k2[rows, cols].astype(jnp.float32) * short.astype(jnp.float32)).astype(jnp.bfloat16)

    def tile_ends(step, groups):
        half, ch, start = place_of(step)
        for group in groups:
            lanes = pl.ds(start + group * LANES, LANES)
            tile = longin[half, ch, :, group * LANES : (group + 1) * LANES].astype(jnp.float32)
            steps = [z8[m : m + 1, lanes] for m in range(MODES)]
            sums = [tile[0:8]] * MODES
            for block in range(1, TILE // 8):
                row = tile[8 * block : 8 * block + 8]
                sums = [s * z + row for s, z in zip(sums, steps)]
            for m, s in enumerate(sums):
                ends[half, m : m + 1, lanes] = jnp.sum(s * zr[m, :, lanes], axis=0, keepdims=True)

    def tap_chunk(ch, carry):
        spectra[ch] = transform(taps[:, pl.ds(pl.multiple_of(ch * WIDE, WIDE), WIDE)])
        return carry

    def send_ends(ch):
        for piece in range(4):
            owner = 4 * ch + piece
            lanes = pl.ds(pl.multiple_of(ch * WIDE, WIDE) + (piece // 2) * LANES, LANES)
            modes = pl.ds(8 * (piece % 2), 8)
            esend[owner] = ends[1, modes, lanes] + kept1 * z128[modes, lanes] * ends[0, modes, lanes]
        for piece in range(4):
            owner = 4 * ch + piece

            @pl.when(owner != me)
            def _():
                pltpu.make_async_remote_copy(
                    src_ref=esend.at[owner], dst_ref=erecv.at[me], send_sem=e_send, recv_sem=e_recv,
                    device_id=(owner, part), device_id_type=MESH).start()

    def side_by_side(step):
        tile_ends(step - 1, (0, 1))
        conv = invert(parts[0], parts[1])
        begun = begin_tile(step + 1)
        finish_tile(step, conv)
        keep_parts(begun)

    def forward_step(step, carry):
        @pl.when(step + 1 >= chunks)
        def _():
            ch = step + 1 - chunks
            wait_bytes(tiles.at[0, ch], halo_recv.at[ch])

        side_by_side(step)

        @pl.when(step - 1 >= chunks)
        def _():
            send_ends(step - 1 - chunks)

        return carry

    lax.fori_loop(0, chunks, tap_chunk, 0)
    last = 2 * chunks - 1
    keep_parts(begin_tile(0))
    first_conv = invert(parts[0], parts[1])
    keep_parts(begin_tile(1))
    finish_tile(0, first_conv)
    lax.fori_loop(1, last, forward_step, 0)
    last_conv = invert(parts[0], parts[1])
    tile_ends(last - 1, (0, 1))
    finish_tile(last, last_conv)
    send_ends(chunks - 2)
    tile_ends(last, (0, 1))
    send_ends(chunks - 1)
    pltpu.make_async_copy(esend.at[me], erecv.at[me], e_recv).start()

    amp[...] = resid[...] * jnp.sqrt(rate[...])
    z1[...] = jnp.exp(-rate[...])

    def lag_taps(ch):
        start = pl.multiple_of(ch * WIDE, WIDE)
        cols = pl.ds(start, WIDE)
        for m in range(MODES):
            zb[m, :, cols] = jnp.exp(-rate[m : m + 1, cols] * sub)
        highs, lows = [], []
        for group in range(2):
            lanes = pl.ds(start + group * LANES, LANES)
            power_of = [amp[m : m + 1, lanes] * zb[m, :, lanes] for m in range(MODES)]
            steps = [z8[m : m + 1, lanes] for m in range(MODES)]
            pieces = []
            for block in range(TILE // 8):
                total = power_of[0]
                for p in power_of[1:]:
                    total = total + p
                pieces.append(total)
                if block < TILE // 8 - 1:
                    power_of = [p * z for p, z in zip(power_of, steps)]
            wide = jnp.concatenate(pieces, axis=0)
            high = wide.astype(jnp.bfloat16)
            highs.append(high)
            lows.append((wide - high.astype(jnp.float32)).astype(jnp.bfloat16))
        return jnp.concatenate(highs, axis=1), jnp.concatenate(lows, axis=1)

    def products(ch, high, low):
        stacked = jnp.concatenate([high, high, low], axis=0)
        spectrum = jnp.dot(ahead[...], stacked, preferred_element_type=jnp.float32)
        return [product_of(transform(longin[half, ch]), spectrum) for half in range(2)]

    def keep_products(made):
        for half in range(2):
            parts[2 * half], parts[2 * half + 1] = made[half]

    def inside_chunk(ch):
        high, low = lag[0], lag[1]
        following = lag_taps(jnp.minimum(ch + 2, chunks - 1))
        made = products(jnp.minimum(ch + 1, chunks - 1), high, low)
        done = [invert(parts[2 * half], parts[2 * half + 1]) for half in range(2)]
        for half in range(2):
            inside[half, ch] = done[half]
        keep_products(made)
        lag[0], lag[1] = following

    opening = lag_taps(0)
    lag[0], lag[1] = lag_taps(1)
    keep_products(products(0, *opening))
    my_cols = pl.ds(pl.multiple_of((me // 2) * LANES, LANES), LANES)
    my_rate = rate[pl.ds(pl.multiple_of(8 * lax.rem(me, 2), 8), 8), my_cols]
    block_decay = jnp.exp(-2.0 * TILE * my_rate)
    slot = me // 4

    def scan_step(n, state):
        ssend[n] = state
        through = flag(jnp.logical_and(n > 0, docs[jnp.maximum(2 * n - 1, 0)] == docs[2 * n + 1]))
        return (block_decay * through) * state + erecv[n]

    def hand_back(step, carry):
        away = 1 + lax.rem(step + seq_count // 2 - 2, seq_count - 1)
        target = lax.rem(me + away, seq_count)
        pltpu.make_async_remote_copy(
            src_ref=ssend.at[target], dst_ref=srecv.at[me], send_sem=s_send, recv_sem=s_recv.at[slot],
            device_id=(target, part), device_id_type=MESH).start()
        return carry

    def middle_chunk(ch, carry):
        @pl.when(ch == 2 + slot // 2)
        def _():
            wait_bytes(erecv, e_recv)
            lax.fori_loop(0, seq_count, scan_step, jnp.zeros((8, LANES), jnp.float32), unroll=8)
            lax.fori_loop(1, seq_count, hand_back, 0)
            pltpu.make_async_copy(ssend.at[me], srecv.at[me], s_recv.at[slot]).start()

        inside_chunk(ch)
        return carry

    lax.fori_loop(0, chunks, middle_chunk, 0)

    power[...] = jnp.zeros_like(power)

    def outward_chunk(ch, carry):
        start = pl.multiple_of(ch * WIDE, WIDE)
        quad = pl.ds(pl.multiple_of(4 * ch, 4), 4)
        wait_bytes(srecv.at[quad], s_recv.at[ch])
        for group in range(2):
            lanes = pl.ds(start + group * LANES, LANES)
            steps = [z8[m : m + 1, lanes] for m in range(MODES)]
            states = [kept0 * srecv[4 * ch + 2 * group + n] for n in range(2)]
            for half in range(2):
                if half == 1:
                    states = [
                        kept1 * (z128[8 * n : 8 * n + 8, lanes] * s + ends[0, 8 * n : 8 * n + 8, lanes])
                        for n, s in enumerate(states)
                    ]
                begun = [amp[8 * n : 8 * n + 8, lanes] * z1[8 * n : 8 * n + 8, lanes] * s for n, s in enumerate(states)]
                waves = [begun[m // 8][m % 8 : m % 8 + 1] * zb[m, :, lanes] for m in range(MODES)]
                for block in range(TILE // 8):
                    total = inside[half, ch, 8 * block : 8 * block + 8, group * LANES : (group + 1) * LANES]
                    for w in waves:
                        total = total + w
                    rows = pl.ds(half * TILE + 8 * block, 8)
                    total = total * q2[rows, lanes].astype(jnp.float32)
                    longout[rows, lanes] = total
                    power[rows, :] = power[rows, :] + total * total
                    if block < TILE // 8 - 1:
                        waves = [w * z for w, z in zip(waves, steps)]
        return carry

    lax.fori_loop(0, chunks, outward_chunk, 0)

    psend[...] = jnp.zeros_like(psend)
    for half in range(2):
        turned = power[half * TILE : (half + 1) * TILE, :].T
        psend[half : half + 1, :] = jnp.sum(turned, axis=0, keepdims=True)
    for step in sorted(range(1, mp_count), key=lambda n: abs(n - mp_count // 2)):
        pltpu.make_async_remote_copy(
            src_ref=psend, dst_ref=precv.at[part], send_sem=p_send, recv_sem=p_recv,
            device_id=(me, lax.rem(part + step, mp_count)), device_id_type=MESH).start()
    precv[part] = psend[...]
    others = pl.ds(0, mp_count - 1)
    wait_bytes(precv.at[others], p_recv)
    total = precv[0]
    for n in range(1, mp_count):
        total = total + precv[n]
    scale = lax.rsqrt(total / (channels * mp_count) + norm_eps)
    for half in range(2):
        column = jnp.broadcast_to(scale[half : half + 1, :], (TILE, LANES)).T
        rows = pl.ds(half * TILE, TILE)
        for group in range(channels // LANES):
            lanes = slice(group * LANES, (group + 1) * LANES)
            outbuf[rows, lanes] = (longout[rows, lanes] * column).astype(jnp.bfloat16)

    wait_bytes(tiles.at[2], halo_send)
    wait_bytes(esend.at[pl.ds(0, seq_count - 1)], e_send)
    wait_bytes(ssend.at[pl.ds(0, seq_count - 1)], s_send)
    wait_bytes(precv.at[others], p_send)


def on_device(mesh_sizes, values, k_first, q_first, k_second, q_second, mr_taps, li_rate, li_residue, tile_docs):
    seq_count, mp_count = mesh_sizes
    rows, channels = values.shape
    chunks = channels // WIDE
    ahead, pair, back = dft_tables()
    f32, bf16 = jnp.float32, jnp.bfloat16
    vmem = pltpu.VMEM
    hbm_spec = pl.BlockSpec(memory_space=pltpu.MemorySpace.HBM)
    big = vmem((rows, channels), bf16)
    modal = vmem((MODES, channels), f32)
    tiles = vmem((seq_count, 8, LANES), f32)
    dma = pltpu.SemaphoreType.DMA
    return pl.pallas_call(
        functools.partial(kernel, seq_count, mp_count),
        out_shape=vmem((rows, channels), bf16),
        in_specs=[pl.BlockSpec(memory_space=pltpu.SMEM)] + [hbm_spec] * 11,
        out_specs=pl.BlockSpec(memory_space=pltpu.VMEM),
        scratch_shapes=[
            big, big, big, big, big,
            vmem((TILE, channels), bf16),
            modal, modal,
            vmem(ahead.shape, bf16),
            vmem(pair.shape, bf16),
            vmem(back.shape, bf16),
            vmem((3, chunks, TILE, WIDE), bf16),
            vmem((2, chunks, TILE, WIDE), bf16),
            vmem((2, chunks, TILE, WIDE), f32),
            vmem((rows, channels), f32),
            modal, modal, modal, modal,
            vmem((MODES, 8, channels), f32),
            vmem((MODES, 8, channels), f32),
            vmem((chunks, 2 * TILE, WIDE), f32),
            vmem((4, 2 * TILE, WIDE), bf16),
            vmem((2, TILE, WIDE), bf16),
            vmem((2,) + pair.shape, bf16),
            vmem((2, MODES, channels), f32),
            tiles, tiles, tiles, tiles,
            vmem((rows, LANES), f32),
            vmem((8, LANES), f32),
            vmem((mp_count, 8, LANES), f32),
            dma((4, chunks)),
            dma((9,)),
            dma,
            dma((chunks,)),
            dma, dma, dma,
            dma((chunks,)),
            dma, dma,
        ],
        compiler_params=pltpu.CompilerParams(
            collective_id=0, has_side_effects=True, vmem_limit_bytes=56 * 1024 * 1024),
    )(tile_docs, values, k_first, q_first, k_second, q_second, mr_taps, li_rate, li_residue,
      jnp.asarray(ahead), jnp.asarray(pair), jnp.asarray(back))


def solution(mesh):
    sizes = (mesh.shape["seq"], mesh.shape["mp"])
    block = P("seq", "mp")
    param = P(None, "mp")
    return jax.shard_map(
        functools.partial(on_device, sizes),
        mesh=mesh,
        in_specs=(block, block, block, block, block, param, param, param, P()),
        out_specs=block,
        check_vma=False,
    )
```
